32 devices in a mesh: mc: 4 (over z), space: 8 (over y, x, core).
Axes of the slice: x: 2, y: 2, z: 4, core: 2. Of those that a mesh axis runs over, the one named last changes fastest.
Arguments:
- orbit_state: float32 [6, 1048576], P(None, ('mc', 'space')), parts along dimension 1, may hold values from -1.3 to 1.3, as said below
- object_props: float32 [3, 1048576], P(None, ('mc', 'space')), parts along dimension 1, may hold values from 0.5 to 2
- density_table: float32 [64], replicated, may hold values from -1 to 1
- block_cube: int32 [8192], P(('mc', 'space')), parts along dimension 0, may hold values from 0 to 1023, as said below
Outputs:
- next_state: float32 [6, 1048576], P(None, ('mc', 'space')), parts along dimension 1
- collision_rate: float32 [1048576], P(('mc', 'space')), parts along dimension 0
The draws below stay inside these ranges and needn't reach their ends.
There are 4 independent parts, one for each index of `mc`. The reference program is written for one: setup_inputs(seed, part) draws one part's arguments, and reference() takes and returns one part's arrays. A program takes and returns all parts, laid end to end along the dimension named above; an argument that names none is the same for every part. Nothing has to cross between parts.
Inputs may be any that keep to these rules, and one draw needn't show every extreme that they name: `orbit_state`: rows 0 to 2 are a position with 1.08 <= |r| <= 1.3, rows 3 to 5 a velocity of speed between 0.86 and 0.98. `block_cube`: cube c is owned by the device of index c // 128 along space. No cube holds more than 4 blocks in all, and in every draw some cube holds exactly 4. The blocks of one device include at most 64 whose cubes have any one owner, and in every draw some owner receives exactly 64 blocks from every device.
All inputs are finite; a program needn't handle non-finite values.
Results may differ from the reference program's by a relative error of at most 0.0003.
Values sent between devices are 32-bit elements; how exact they have to be, the bound alone decides.
No kernel may reach another device: no remote copies, remote signals or barrier semaphores. Data moves between devices by JAX's collectives and lax.ppermute only.
A program may use at most 64 MiB of HBM per device.

```python
import math
import jax
import jax.numpy as jnp
from jax import lax

BLK = 128
BLK_DEV = 256
MOST = 4
SUB = 16
NTAB = 64
CAP = 64
CUBE_DEV = 128
NBLOCKS = 2048
OBJECTS = 262144
N_SPACE = 8


def draw_orbit_state(key, part):
    key_alt, key_dir, key_tan, key_speed, key_radial = jax.random.split(jax.random.fold_in(key, 11), 5)
    height = jax.random.uniform(key_alt, (OBJECTS,), jnp.float32, 0.08, 0.3)
    normal_dir = jax.random.normal(key_dir, (3, OBJECTS), jnp.float32)
    unit_dir = normal_dir / jnp.sqrt(jnp.sum(normal_dir * normal_dir, axis=0) + 1e-12)
    tangent = jax.random.normal(key_tan, (3, OBJECTS), jnp.float32)
    tangent = tangent - jnp.sum(tangent * unit_dir, axis=0) * unit_dir
    tangent = tangent / jnp.sqrt(jnp.sum(tangent * tangent, axis=0) + 1e-12)
    radius = 1.0 + height
    circular = jax.random.uniform(key_speed, (OBJECTS,), jnp.float32, 0.99, 1.01) / jnp.sqrt(radius)
    radial = 0.01 * jnp.clip(jax.random.normal(key_radial, (OBJECTS,), jnp.float32), -3.0, 3.0)
    position = radius * unit_dir
    velocity = circular * (tangent + radial * unit_dir)
    return jnp.concatenate([position, velocity], axis=0)


def draw_block_cube(key, part):
    base_key = jax.random.fold_in(key, 29)
    key_hot, key_pick, key_order, key_slot = jax.random.split(base_key, 4)
    hot_owner = jax.random.randint(key_hot, (), 0, N_SPACE)
    other_width = (N_SPACE - 1) * CAP
    others = jnp.arange(other_width) // CAP
    others = others + (others >= hot_owner).astype(jnp.int32)
    pick_score = jax.random.randint(key_pick, (N_SPACE, other_width), 0, 1 << 16) * other_width + jnp.arange(other_width)[None, :]
    picked = others[jnp.argsort(pick_score, axis=1)[:, :BLK_DEV - CAP]]
    owners = jnp.concatenate([jnp.full((N_SPACE, CAP), hot_owner, jnp.int32), picked.astype(jnp.int32)], axis=1)
    order_score = jax.random.randint(key_order, (N_SPACE, BLK_DEV), 0, 1 << 16) * BLK_DEV + jnp.arange(BLK_DEV)[None, :]
    owners = jnp.take_along_axis(owners, jnp.argsort(order_score, axis=1), axis=1).reshape(NBLOCKS)
    onehot = (owners[:, None] == jnp.arange(N_SPACE)[None, :]).astype(jnp.int32)
    owner_rank = jnp.sum((jnp.cumsum(onehot, axis=0) - onehot) * onehot, axis=1)
    slot_total = CUBE_DEV * MOST
    slot_score = jax.random.randint(key_slot, (N_SPACE, slot_total), 0, 1 << 16) * slot_total + jnp.arange(slot_total)[None, :]
    slot_perm = jnp.argsort(slot_score, axis=1)
    local_cube = slot_perm[owners, owner_rank] // MOST
    return (owners * CUBE_DEV + local_cube).astype(jnp.int32)


def steps_of(key, shape, cuts, least, high):
    factor_of = 1.0
    for dim, shards_of in cuts:
        steps = jax.random.uniform(jax.random.fold_in(jax.random.fold_in(key, 6), dim), (shards_of,), jnp.float32, least / len(cuts), high / len(cuts))
        factor_of = factor_of * jnp.repeat(jnp.exp(steps), shape[dim] // shards_of).reshape((-1,) + (1,) * (len(shape) - 1 - dim))
    return factor_of


def setup_inputs(seed: int = 0, part: int = 0) -> dict:
    key_list = jax.random.split(jax.random.key(seed), 5)
    part_keys = jax.random.split(jax.random.fold_in(key_list[4], part), 5)
    return {
        "orbit_state": draw_orbit_state(jax.random.fold_in(jax.random.fold_in(key_list[4], part), 71), part),
        "object_props": jnp.clip(jnp.exp(math.log(2.0) - 1.3862944 * jax.random.uniform(part_keys[1], (3, OBJECTS), jnp.float32) ** steps_of(part_keys[1], (3, OBJECTS), ((1, 8),), -0.2, 0.2)), 0.5, 2.0),
        "density_table": jnp.clip(jax.random.uniform(key_list[2], (NTAB,), jnp.float32, -1.0, 1.0), -1.0, 1.0),
        "block_cube": draw_block_cube(jax.random.fold_in(jax.random.fold_in(key_list[4], part), 71), part),
    }


TIME_STEP = 0.2
EARTH_SPIN = 0.0588
J2_COEF = 0.00108263
DRAG_SCALE = 0.008
SCALE_HEIGHT = 0.1
TABLE_TOP = 0.4
SPEED_FLOOR = 0.04

def propagate(orbit_part, prop_part, density_table):
    position = orbit_part[0:3]
    velocity = orbit_part[3:6]
    ballistic = prop_part[2]
    alt_grid = jnp.arange(NTAB).astype(density_table.dtype)
    for substep in range(SUB):
        radius_sq = lax.optimization_barrier(jnp.sum(position * position, axis=0))
        radius = jnp.sqrt(radius_sq)
        height = radius - 1.0
        table_coord = height * ((NTAB - 1) / TABLE_TOP)
        hat_weights = jnp.maximum(0.0, 1.0 - jnp.abs(table_coord[None, :] - alt_grid[:, None]))
        log_density = jnp.dot(density_table[None, :], hat_weights, precision=lax.Precision.HIGHEST)[0] - height / SCALE_HEIGHT
        density = DRAG_SCALE * jnp.exp(log_density)
        relative = jnp.stack([velocity[0] + EARTH_SPIN * position[1], velocity[1] - EARTH_SPIN * position[0], velocity[2]])
        air_speed = jnp.sqrt(lax.optimization_barrier(jnp.sum(relative * relative, axis=0)))
        inv_cube = 1.0 / (radius_sq * radius)
        polar_ratio = position[2] * position[2] / radius_sq
        oblate_factor = 1.5 * J2_COEF / (radius_sq * radius_sq * radius)
        shape_term = jnp.stack([1.0 - 5.0 * polar_ratio, 1.0 - 5.0 * polar_ratio, 3.0 - 5.0 * polar_ratio])
        acceleration = -position * inv_cube - oblate_factor * position * shape_term - density * ballistic * air_speed * relative
        velocity = velocity + TIME_STEP * acceleration
        position = position + TIME_STEP * velocity
    return jnp.concatenate([position, velocity], axis=0)

def propagate_all(orbit_state, object_props, density_table):
    total_count = orbit_state.shape[1]
    span_width = math.gcd(total_count, 4096)
    groups = total_count // span_width
    stacked = orbit_state.reshape(6, groups, span_width).transpose(1, 0, 2)
    prop_stack = object_props.reshape(3, groups, span_width).transpose(1, 0, 2)
    advanced = lax.map(lambda packed: propagate(packed[0], packed[1], density_table), (stacked, prop_stack))
    return advanced.transpose(1, 0, 2).reshape(6, total_count)

def group_rates(group_ids, partners, partner_ok, velocity, radius, weight):
    group_size = group_ids.shape[0]
    own_vel = velocity[:, group_ids]
    peer_vel = velocity[:, partners].reshape(3, group_size, MOST * BLK)
    diff_sq = jnp.zeros((group_size, BLK, MOST * BLK), velocity.dtype)
    for component in range(3):
        gap = own_vel[component][:, :, None] - peer_vel[component][:, None, :]
        diff_sq = diff_sq + gap * gap
    own_rad = radius[group_ids][:, :, None]
    peer_rad = radius[partners].reshape(group_size, 1, MOST * BLK)
    peer_wt = weight[partners].reshape(group_size, 1, MOST * BLK)
    same_block = jnp.repeat(partners == group_ids[:, None], BLK, axis=1)[:, None, :]
    column_ok = jnp.repeat(partner_ok, BLK, axis=1)[:, None, :]
    same_index = (jnp.arange(BLK)[:, None] == (jnp.arange(MOST * BLK) % BLK)[None, :])[None, :, :]
    keep_mask = column_ok & jnp.logical_not(same_block & same_index)
    pair_term = jnp.where(keep_mask, peer_wt * (own_rad + peer_rad) ** 2 * jnp.sqrt(diff_sq + SPEED_FLOOR), 0.0)
    return weight[group_ids] * lax.optimization_barrier(jnp.sum(pair_term, axis=2)) / (MOST * BLK)

def reference(orbit_state, object_props, density_table, block_cube):
    next_state = propagate_all(orbit_state, object_props, density_table)
    velocity = next_state[3:6].reshape(3, NBLOCKS, BLK)
    radius = object_props[0].reshape(NBLOCKS, BLK)
    weight = object_props[1].reshape(NBLOCKS, BLK)
    block_index = jnp.arange(NBLOCKS).astype(jnp.int32)

    def one_group(first_block):
        group_ids = (first_block + jnp.arange(16)).astype(jnp.int32)
        same_cube = block_cube[group_ids][:, None] == block_cube[None, :]
        scores = jnp.where(same_cube, 2 * NBLOCKS - block_index[None, :], NBLOCKS - block_index[None, :]).astype(jnp.int32)
        values, partners = lax.top_k(scores, MOST)
        return group_rates(group_ids, partners.astype(jnp.int32), values > NBLOCKS, velocity, radius, weight)
    block_rates = lax.map(one_group, jnp.arange(0, NBLOCKS, 16).astype(jnp.int32))
    return (next_state, block_rates.reshape(OBJECTS))
```

```python
import functools

import jax
import jax.numpy as jnp
from jax import lax
from jax.experimental import pallas as pl
from jax.experimental.pallas import tpu as pltpu
from jax.sharding import PartitionSpec as P

LANES = 128
MOST = 4
SUB = 16
NTAB = 64

TIME_STEP = 0.2
EARTH_SPIN = 0.0588
J2_COEF = 0.00108263
DRAG_SCALE = 0.008
SCALE_HEIGHT = 0.1
TABLE_TOP = 0.4
SPEED_FLOOR = 0.04

F32 = jnp.float32
BF = jnp.bfloat16


def substep(state, ballistic, table, slopes):
    x, y, z, vx, vy, vz = state
    zz = z * z
    radius_sq = x * x + y * y + zz
    inv = lax.rsqrt(radius_sq)
    height = radius_sq * inv - 1.0
    coord = jnp.clip(height * ((NTAB - 1) / TABLE_TOP), -1.0, float(NTAB))
    cell = jnp.floor(coord)
    index = cell.astype(jnp.int32) + 1
    base = jnp.take_along_axis(table, index, axis=1, mode="promise_in_bounds")
    slope = jnp.take_along_axis(slopes, index, axis=1, mode="promise_in_bounds")
    log_density = base + (coord - cell) * slope - height * (1.0 / SCALE_HEIGHT)
    ux = vx + EARTH_SPIN * y
    uy = vy - EARTH_SPIN * x
    air_sq = ux * ux + uy * uy + vz * vz
    drag = (TIME_STEP * DRAG_SCALE) * jnp.exp(log_density) * (ballistic * jnp.sqrt(air_sq))
    inv_sq = inv * inv
    inv_cube = inv_sq * inv
    oblate = (1.5 * J2_COEF * TIME_STEP) * (inv_cube * inv_sq)
    pull = TIME_STEP * inv_cube + oblate * (1.0 - 5.0 * (zz * inv_sq))
    pull_z = pull + 2.0 * oblate
    vx = vx - x * pull - drag * ux
    vy = vy - y * pull - drag * uy
    vz = vz - z * pull_z - drag * vz
    return (x + TIME_STEP * vx, y + TIME_STEP * vy, z + TIME_STEP * vz, vx, vy, vz)


def propagate_kernel(table_ref, orbit_ref, props_ref, next_ref, vel_a, vel_b, tiles, drags, *, group, unroll):
    blocks = orbit_ref.shape[1] // LANES
    half = blocks // 2
    for b in range(blocks):
        tiles[pl.ds(8 * b, 6), :] = orbit_ref[:, pl.ds(b * LANES, LANES)]
        drags[pl.ds(8 * b, 1), :] = props_ref[pl.ds(2, 1), pl.ds(b * LANES, LANES)]
    rows = group * 8
    table = jnp.broadcast_to(table_ref[pl.ds(0, 1), :], (rows, LANES))
    slopes = jnp.broadcast_to(table_ref[pl.ds(1, 1), :], (rows, LANES))

    def chunk(i, start, out_ref):
        base = pl.multiple_of((start + i * rows) * 8, 8 * rows)
        state = tuple(tiles[pl.ds(base + c, rows, stride=8), :] for c in range(6))
        ballistic = drags[pl.ds(base, rows, stride=8), :]
        state = lax.fori_loop(
            0, SUB, lambda k, s: substep(s, ballistic, table, slopes), state, unroll=unroll
        )
        for c in range(6):
            tiles[pl.ds(base + c, rows, stride=8), :] = state[c]
        for c in range(3):
            out_ref[pl.ds(pl.multiple_of(c * half + i * rows, 8), rows), :] = state[3 + c]

    for start, out_ref in ((0, vel_a), (half, vel_b)):
        for i in range(half // rows):
            chunk(i, start, out_ref)
    for b in range(blocks):
        next_ref[:, pl.ds(b * LANES, LANES)] = tiles[pl.ds(8 * b, 6), :]


def propagate(table, orbit_state, object_props):
    count = orbit_state.shape[1]
    blocks = count // LANES
    vel = jax.ShapeDtypeStruct((3 * blocks // 2, LANES), F32)
    return pl.pallas_call(
        functools.partial(propagate_kernel, group=16, unroll=2),
        out_shape=(jax.ShapeDtypeStruct((6, count), F32), vel, vel),
        scratch_shapes=[pltpu.VMEM((blocks * 8, LANES), F32), pltpu.VMEM((blocks * 8, LANES), F32)],
        name="propagate",
    )(table, orbit_state, object_props)


def split3(a):
    high = a.astype(BF).astype(F32)
    rest = a - high
    mid = rest.astype(BF).astype(F32)
    return high, mid, rest - mid


def rates_kernel(order_ref, parts_ref, most_ref, *refs, pieces, half, srows, group):
    s_in = refs[: 2 * pieces]
    v_in = refs[2 * pieces : 4 * pieces]
    out_ref, gs, gv, lhs_ref, cols, sem = refs[4 * pieces :]
    blocks = 2 * half
    vrows = 3 * half
    copies = []
    row_s = row_v = 0
    for a, b in zip(s_in, v_in):
        copies.append(pltpu.make_async_copy(a, gs.at[pl.ds(row_s, a.shape[0]), :], sem.at[len(copies)]))
        copies.append(pltpu.make_async_copy(b, gv.at[pl.ds(row_v, b.shape[0]), :], sem.at[len(copies)]))
        row_s += a.shape[0]
        row_v += b.shape[0]
    for c in copies:
        c.start()
    gs[pl.ds(row_s, srows), :] = jnp.zeros((srows, LANES), F32)
    gv[pl.ds(row_v, vrows), :] = jnp.zeros((vrows, LANES), F32)
    for c in copies:
        c.wait()
    units = row_s // srows // 2
    sub = lax.broadcasted_iota(jnp.int32, (8, LANES), 0)
    lane = lax.broadcasted_iota(jnp.int32, (LANES, LANES), 1)
    one = jnp.ones((8, LANES), F32)

    def pick(rows):
        out = rows[7]
        for k in range(6, -1, -1):
            out = jnp.where(sub == k, rows[k], out)
        return out

    def load(ref, r):
        return jnp.broadcast_to(ref[pl.ds(r, 1), :], (8, LANES))

    def own_features(b, carry):
        u = (b // half) * units
        r = b % half
        vx, vy, vz = (load(gv, u * vrows + c * half + r) for c in range(3))
        rad = load(gs, u * srows + r)
        speed_sq = vx * vx + vy * vy + vz * vz
        own = pick([-2.0 * vx, -2.0 * vy, -2.0 * vz, one, speed_sq, rad * rad, 2.0 * rad, one])
        high, mid, low = split3(own)
        rows = jnp.concatenate([high, high, mid, mid, high, low, jnp.zeros((80, LANES), F32)], 0)
        lhs_ref[pl.ds(pl.multiple_of(b * LANES, LANES), LANES), :] = rows.T.astype(BF)
        return carry

    lax.fori_loop(0, blocks, own_features, 0, unroll=2)
    pad = jnp.zeros((80, LANES), BF)

    def mate_features(p):
        u = p // half
        r = p % half
        vx, vy, vz = (load(gv, u * vrows + c * half + r) for c in range(3))
        rad = load(gs, u * srows + r)
        wt = load(gs, u * srows + half + r)
        wr = wt * rad
        speed_sq = vx * vx + vy * vy + vz * vz
        mate = pick([vx, vy, vz, speed_sq + SPEED_FLOOR, one, wt, wr, wr * rad])
        out = []
        for keep in (sub < 5, sub >= 5):
            high, mid, low = split3(jnp.where(keep, mate, 0.0))
            top = jnp.concatenate([high, mid], 0).astype(BF)
            bottom = jnp.concatenate([low, high], 0).astype(BF)
            out.append(jnp.concatenate([top, top, bottom, pad], 0))
        return out

    def run(g, count):
        for k in range(group):
            slot = g * group + k
            b = order_ref[slot]
            lhs = lhs_ref[pl.ds(pl.multiple_of(b * LANES, LANES), LANES), :]
            acc = None
            for p in range(count):
                gap_rows, size_rows = mate_features(parts_ref[slot * MOST + p])
                gap = jnp.dot(lhs, gap_rows, preferred_element_type=F32)
                size = jnp.dot(lhs, size_rows, preferred_element_type=F32)
                gap = jnp.maximum(gap, SPEED_FLOOR)
                term = size * (gap * lax.rsqrt(gap))
                acc = term if acc is None else acc + term
            col = jnp.sum(acc, axis=1, keepdims=True)
            tile = b // LANES
            at = pl.ds(pl.multiple_of(tile * LANES, LANES), LANES)
            cols[at, :] = jnp.where(lane == b - tile * LANES, col, cols[at, :])

    def step(g, carry):
        most = most_ref[g]
        for count in range(1, MOST + 1):

            @pl.when(most == count)
            def _():
                run(g, count)

        return carry

    lax.fori_loop(0, blocks // group, step, 0)
    for b in range(0, blocks, LANES):
        total = cols[pl.ds(b, LANES), :].T
        at = (b // half) * units * srows + b % half
        rad = gs[pl.ds(at, LANES), :]
        wt = gs[pl.ds(at + half, LANES), :]
        self_term = (4.0 * SPEED_FLOOR**0.5) * wt * rad * rad
        out_ref[pl.ds(b, LANES), :] = wt * (total - self_term) * (1.0 / (MOST * LANES))


def rates(order, parts, most, s_pieces, v_pieces, half, srows, group):
    pieces = len(s_pieces) // 2
    total_s = sum(a.shape[0] for a in s_pieces) + srows
    total_v = sum(a.shape[0] for a in v_pieces) + 3 * half
    return pl.pallas_call(
        functools.partial(rates_kernel, pieces=pieces, half=half, srows=srows, group=group),
        in_specs=[pl.BlockSpec(memory_space=pltpu.SMEM)] * 3
        + [pl.BlockSpec(memory_space=pl.ANY)] * (4 * pieces),
        out_shape=jax.ShapeDtypeStruct((2 * half, LANES), F32),
        scratch_shapes=[
            pltpu.VMEM((total_s, LANES), F32),
            pltpu.VMEM((total_v, LANES), F32),
            pltpu.VMEM((2 * half * LANES, LANES), BF),
            pltpu.VMEM((2 * half, LANES), F32),
            pltpu.SemaphoreType.DMA((4 * pieces,)),
        ],
        name="rates",
    )(order, parts, most, *s_pieces, *v_pieces)


def find_partners(own, every, group):
    blocks = own.shape[0]
    total = every.shape[0]
    index = jnp.arange(total, dtype=jnp.int32)[None, :]
    same = own[:, None] == every[None, :]
    last = jnp.full((blocks,), -1, jnp.int32)
    found = []
    for _ in range(MOST):
        last = jnp.min(jnp.where(same & (index > last[:, None]), index, total), axis=1)
        found.append(last)
    parts = jnp.stack(found, 1)
    count = jnp.sum((parts < total).astype(jnp.int32), axis=1)
    ids = jnp.arange(blocks, dtype=jnp.int32)
    ahead = (count[None, :] > count[:, None]) | (
        (count[None, :] == count[:, None]) & (ids[None, :] < ids[:, None])
    )
    rank = jnp.sum(ahead.astype(jnp.int32), axis=1)
    at_slot = (rank[None, :] == ids[:, None]).astype(jnp.int32)
    order = jnp.sum(at_slot * ids[None, :], axis=1)
    parts = jnp.sum(at_slot[:, :, None] * parts[None], axis=1)
    most = jnp.sum(at_slot * count[None, :], axis=1)[::group]
    return order, parts.reshape(-1), most


def exchange(own_a, own_b, size):
    bits = [1 << k for k in range(size.bit_length() - 2, -1, -1)]
    swapped = bits[1::-1] + bits[2:]

    def send(a, bit):
        return lax.ppermute(a, "space", [(i, i ^ bit) for i in range(size)])

    pieces_a, pieces_b = [own_a], [own_b]
    for bit_a, bit_b in zip(bits, swapped):
        out_a = jnp.concatenate(pieces_a, 0) if len(pieces_a) > 1 else own_a
        out_b = jnp.concatenate(pieces_b, 0) if len(pieces_b) > 1 else own_b
        pieces_a.append(send(out_a, bit_a))
        pieces_b.append(send(out_b, bit_b))
    return pieces_a, pieces_b


def on_device(orbit_state, object_props, density_table, block_cube):
    size = lax.axis_size("space")
    blocks = block_cube.shape[0]
    half = blocks // 2
    group = 8
    table = jnp.pad(density_table, (1, LANES - NTAB - 1))
    table = jnp.stack([table, jnp.pad(density_table, (0, LANES - NTAB)) - table])
    cube_rows = -(-half // (8 * LANES)) * 8
    srows = 2 * half + cube_rows
    planes = object_props[0:2].reshape(2, blocks, LANES)
    cubes = block_cube.astype(F32)

    def static(lo):
        ids = jnp.pad(cubes[lo : lo + half], (0, cube_rows * LANES - half))
        rows = planes[:, lo : lo + half].reshape(2 * half, LANES)
        return jnp.concatenate([rows, ids.reshape(cube_rows, LANES)], 0)

    s_a, s_b = exchange(static(0), static(half), size)
    every = jnp.concatenate(
        [a.reshape(-1, srows, LANES)[:, 2 * half :].reshape(-1, cube_rows * LANES)[:, :half] for a in s_a + s_b]
    ).reshape(-1)
    next_state, vel_a, vel_b = propagate(table, orbit_state, object_props)
    v_a, v_b = exchange(vel_a, vel_b, size)
    order, parts, most = find_partners(cubes, every, group)
    out = rates(order, parts, most, s_a + s_b, v_a + v_b, half, srows, group)
    return (next_state, out.reshape(blocks * LANES))


def solution(mesh):
    placed = (P(None, ("mc", "space")), P(None, ("mc", "space")), P(), P(("mc", "space")))
    return jax.shard_map(
        on_device,
        mesh=mesh,
        in_specs=placed,
        out_specs=(P(None, ("mc", "space")), P(("mc", "space"))),
        check_vma=False,
    )
```

```python
import functools

import jax
import jax.numpy as jnp
from jax import lax
from jax.experimental import pallas as pl
from jax.experimental.pallas import tpu as pltpu
from jax.sharding import PartitionSpec as P

LANES = 128
MOST = 4
SUB = 16
NTAB = 64

TIME_STEP = 0.2
EARTH_SPIN = 0.0588
J2_COEF = 0.00108263
DRAG_SCALE = 0.008
SCALE_HEIGHT = 0.1
TABLE_TOP = 0.4
SPEED_FLOOR = 0.04

F32 = jnp.float32
BF = jnp.bfloat16


def unit_rows(blocks):
    return 5 * blocks + -(-blocks // (8 * LANES)) * 8


def substep(state, ballistic, table, slopes):
    x, y, z, vx, vy, vz = state
    zz = z * z
    radius_sq = x * x + y * y + zz
    inv = lax.rsqrt(radius_sq)
    height = radius_sq * inv - 1.0
    coord = jnp.clip(height * ((NTAB - 1) / TABLE_TOP), -1.0, float(NTAB))
    cell = jnp.floor(coord)
    index = cell.astype(jnp.int32) + 1
    base = jnp.take_along_axis(table, index, axis=1, mode="promise_in_bounds")
    slope = jnp.take_along_axis(slopes, index, axis=1, mode="promise_in_bounds")
    log_density = base + (coord - cell) * slope - height * (1.0 / SCALE_HEIGHT)
    ux = vx + EARTH_SPIN * y
    uy = vy - EARTH_SPIN * x
    air_sq = ux * ux + uy * uy + vz * vz
    drag = (TIME_STEP * DRAG_SCALE) * jnp.exp(log_density) * (ballistic * jnp.sqrt(air_sq))
    inv_sq = inv * inv
    inv_cube = inv_sq * inv
    oblate = (1.5 * J2_COEF * TIME_STEP) * (inv_cube * inv_sq)
    pull = TIME_STEP * inv_cube + oblate * (1.0 - 5.0 * (zz * inv_sq))
    pull_z = pull + 2.0 * oblate
    vx = vx - x * pull - drag * ux
    vy = vy - y * pull - drag * uy
    vz = vz - z * pull_z - drag * vz
    return (x + TIME_STEP * vx, y + TIME_STEP * vy, z + TIME_STEP * vz, vx, vy, vz)


def propagate_kernel(table_ref, orbit_ref, props_ref, cube_ref, next_ref, unit_ref, tiles, props, lut, *, group, unroll):
    blocks = orbit_ref.shape[1] // LANES
    rows = group * 8
    for b in range(blocks):
        tiles[pl.ds(8 * b, 6), :] = orbit_ref[:, pl.ds(b * LANES, LANES)]
        props[pl.ds(8 * b, 3), :] = props_ref[:, pl.ds(b * LANES, LANES)]
    lut[...] = jnp.zeros((8, LANES), F32)
    lut[pl.ds(0, 1), pl.ds(0, NTAB)] = table_ref[...]
    knots = jnp.broadcast_to(lut[pl.ds(0, 1), :], (8, LANES))
    table = pltpu.roll(knots, 1, 1)
    slopes = jnp.tile(knots - table, (group, 1))
    table = jnp.tile(table, (group, 1))
    unit_ref[pl.ds(5 * blocks, unit_ref.shape[0] - 5 * blocks), :] = jnp.zeros(
        (unit_ref.shape[0] - 5 * blocks, LANES), F32
    )
    unit_ref[pl.ds(5 * blocks, blocks // LANES), :] = cube_ref[...].astype(F32)
    for i in range(blocks // rows):
        base = 8 * rows * i
        state = tuple(tiles[pl.ds(base + c, rows, stride=8), :] for c in range(6))
        radius, weight, ballistic = (props[pl.ds(base + c, rows, stride=8), :] for c in range(3))
        state = lax.fori_loop(
            0, SUB, lambda k, s: substep(s, ballistic, table, slopes), state, unroll=unroll
        )
        for c in range(6):
            tiles[pl.ds(base + c, rows, stride=8), :] = state[c]
        for c, plane in enumerate((*state[3:], radius, weight)):
            unit_ref[pl.ds(c * blocks + i * rows, rows), :] = plane
    for b in range(blocks):
        next_ref[:, pl.ds(b * LANES, LANES)] = tiles[pl.ds(8 * b, 6), :]


def propagate(density_table, orbit_state, object_props, block_cube):
    count = orbit_state.shape[1]
    blocks = count // LANES
    return pl.pallas_call(
        functools.partial(propagate_kernel, group=16, unroll=2),
        out_shape=(
            jax.ShapeDtypeStruct((6, count), F32),
            jax.ShapeDtypeStruct((unit_rows(blocks), LANES), F32),
        ),
        scratch_shapes=[
            pltpu.VMEM((blocks * 8, LANES), F32),
            pltpu.VMEM((blocks * 8, LANES), F32),
            pltpu.VMEM((8, LANES), F32),
        ],
        name="propagate",
    )(density_table.reshape(1, NTAB), orbit_state, object_props, block_cube.reshape(blocks // LANES, LANES))


def split3(a):
    high = a.astype(BF).astype(F32)
    rest = a - high
    mid = rest.astype(BF).astype(F32)
    return high, mid, rest - mid


def whole_tiles(rows):
    extra = -len(rows) % 8
    return jnp.concatenate([*rows, *([jnp.zeros((extra, LANES), F32)] if extra else [])], 0)


def partner_table(own_ids, mate_ids, most):
    none = float(len(mate_ids) * LANES)
    sub = lax.broadcasted_iota(jnp.int32, (LANES, LANES), 0).astype(F32)
    lane = lax.broadcasted_iota(jnp.int32, (LANES, LANES), 1).astype(F32)
    cols = whole_tiles(mate_ids).T
    found = []
    for own in own_ids:
        places = [
            jnp.where(cols[:, t : t + 1] == own, sub + float(t * LANES), none) for t in range(len(mate_ids))
        ]
        last = jnp.full((1, LANES), -1.0, F32)
        hits = []
        for _ in range(most):
            best = None
            for place in places:
                later = jnp.where(place > last, place, none)
                best = later if best is None else jnp.minimum(best, later)
            last = jnp.min(best, axis=0, keepdims=True)
            hits.append(last)
        found.append(hits)
    counts = [sum((hit < none).astype(F32) for hit in hits) for hits in found]
    rows = counts + [hit for hits in found for hit in hits]
    turned = whole_tiles(rows).T
    halves = len(own_ids)
    ordered = [[0.0] * (most + 2) for _ in range(halves)]
    for h in range(halves):
        count = turned[:, h : h + 1]
        ahead = 0.0
        for g in range(halves):
            before = (lane + float(g * LANES)) < (sub + float(h * LANES))
            ahead = ahead + jnp.where((counts[g] > count) | ((counts[g] == count) & before), 1.0, 0.0)
        rank = jnp.sum(ahead, axis=1, keepdims=True)
        for q in range(halves):
            here = rank == lane + float(q * LANES)
            take = lambda v: jnp.sum(jnp.where(here, v, 0.0), axis=0, keepdims=True)
            ordered[q][0] += take(sub + float(h * LANES))
            ordered[q][1] += take(count)
            for p in range(most):
                at = halves + h * most + p
                ordered[q][2 + p] += take(turned[:, at : at + 1])
    rows = [ordered[q][k] for k in range(most + 2) for q in range(halves)]
    return whole_tiles(rows).astype(jnp.int32)


def pairs_kernel(*refs, arrays, first, last, most, group):
    own_ref, *mate_refs = refs[: 1 + arrays]
    refs = refs[1 + arrays :]
    if not first:
        prev_ref, *refs = refs
    out_ref, raw, own_tiles, mate_tiles, cols, table_vmem, table, sem, table_sem = refs
    blocks = out_ref.shape[0]
    rows = unit_rows(blocks)
    halves = blocks // LANES
    copies = []
    at = 0
    for k, ref in enumerate((own_ref, *mate_refs)):
        copies.append(pltpu.make_async_copy(ref, raw.at[pl.ds(at, ref.shape[0]), :], sem.at[k]))
        at += ref.shape[0]
    for copy in copies:
        copy.start()
    units = list(range(0 if first else 1, at // rows))
    cols[...] = jnp.zeros(cols.shape, F32)
    mate_tiles[pl.ds(len(units) * blocks * 8, 8), :] = jnp.zeros((8, LANES), F32)
    for copy in copies:
        copy.wait()

    def ids(unit):
        return [raw[pl.ds(unit * rows + 5 * blocks + h, 1), :] for h in range(halves)]

    table_vmem[...] = partner_table(ids(0), [row for u in units for row in ids(u)], most)
    to_smem = pltpu.make_async_copy(table_vmem, table, table_sem.at[0])
    to_smem.start()
    one = jnp.ones((8, LANES), F32)

    def planes(unit, i):
        base = unit * rows + i * 8
        at = [pl.multiple_of(base + c * blocks, 8) for c in range(5)]
        return [raw[pl.ds(a, 8), :] for a in at]

    def own_tile(i, carry):
        vx, vy, vz, rad, _ = planes(0, i)
        speed_sq = vx * vx + vy * vy + vz * vz
        for k, row in enumerate((-2.0 * vx, -2.0 * vy, -2.0 * vz, one, speed_sq, rad * rad, 2.0 * rad, one)):
            own_tiles[pl.ds(i * 64 + k, 8, stride=8), :] = row
        return carry

    lax.fori_loop(0, blocks // 8, own_tile, 0, unroll=4)
    for n, unit in enumerate(units):

        def mate_tile(i, carry):
            vx, vy, vz, rad, wt = planes(unit, i)
            speed_sq = vx * vx + vy * vy + vz * vz + SPEED_FLOOR
            for k, row in enumerate((vx, vy, vz, speed_sq, one, wt, wt * rad, wt * rad * rad)):
                mate_tiles[pl.ds(n * blocks * 8 + i * 64 + k, 8, stride=8), :] = row
            return carry

        lax.fori_loop(0, blocks // 8, mate_tile, 0, unroll=4)
    to_smem.wait()
    lane = lax.broadcasted_iota(jnp.int32, (LANES, LANES), 1)
    is_gap = lax.broadcasted_iota(jnp.int32, (16, LANES), 0) % 8 < 5
    blank = jnp.zeros((16, LANES), BF)
    pad = jnp.zeros((80, LANES), BF)

    def stack(a, b):
        return jnp.concatenate([a, b], 0).astype(BF)

    def run(q, place, count):
        for k in range(group):
            b = table[q, place + k]
            high, mid, low = split3(own_tiles[pl.ds(pl.multiple_of(b * 8, 8), 8), :])
            lhs = jnp.concatenate([stack(high, high), stack(mid, mid), stack(high, low), pad], 0).T
            acc = None
            for p in range(count):
                mate = table[(2 + p) * halves + q, place + k]
                high, mid, low = split3(mate_tiles[pl.ds(pl.multiple_of(mate * 8, 8), 8), :])
                top, bottom = stack(high, mid), stack(low, high)
                sides = []
                for keep in (is_gap, jnp.logical_not(is_gap)):
                    upper = jnp.where(keep, top, blank)
                    sides.append(jnp.concatenate([upper, upper, jnp.where(keep, bottom, blank), pad], 0))
                both = jnp.dot(lhs, jnp.concatenate(sides, 1), preferred_element_type=F32)
                gap = jnp.maximum(both[:, :LANES], SPEED_FLOOR)
                term = both[:, LANES:] * (gap * lax.rsqrt(gap))
                acc = term if acc is None else acc + term
            total = jnp.broadcast_to(jnp.sum(acc, axis=1, keepdims=True), (LANES, LANES))
            at = pl.multiple_of(jnp.bitwise_and(b, -LANES), LANES)
            pltpu.store(cols.at[pl.ds(at, LANES), :], total, mask=lane == jnp.bitwise_and(b, LANES - 1))

    def step(g, carry):
        q = g // (LANES // group)
        place = (g % (LANES // group)) * group
        longest = table[halves + q, place]
        for count in range(1, most + 1):

            @pl.when(longest == count)
            def _():
                run(q, place, count)

        return carry

    lax.fori_loop(0, blocks // group, step, 0)
    for h in range(halves):
        at = pl.ds(h * LANES, LANES)
        total = cols[at, :].T
        rad = raw[pl.ds(3 * blocks + h * LANES, LANES), :]
        wt = raw[pl.ds(4 * blocks + h * LANES, LANES), :]
        if first:
            total = total - (4.0 * SPEED_FLOOR**0.5) * wt * rad * rad
        else:
            total = total + prev_ref[at, :]
        if last:
            total = wt * total * (1.0 / (MOST * LANES))
        out_ref[at, :] = total


def pairs(own, mates, prev, last):
    rows = own.shape[0]
    blocks = rows // 5 // LANES * LANES
    first = prev is None
    most = MOST if first else MOST - 1
    total = sum(a.shape[0] for a in (own, *mates)) // rows
    tiles = (total if first else total - 1) * blocks + 1
    table = -(-(most + 2) * (blocks // LANES) // 8) * 8
    return pl.pallas_call(
        functools.partial(pairs_kernel, arrays=len(mates), first=first, last=last, most=most, group=16),
        in_specs=[pl.BlockSpec(memory_space=pl.ANY)] * (1 + len(mates))
        + ([] if first else [pl.BlockSpec(memory_space=pltpu.VMEM)]),
        out_shape=jax.ShapeDtypeStruct((blocks, LANES), F32),
        scratch_shapes=[
            pltpu.VMEM((total * rows, LANES), F32),
            pltpu.VMEM((blocks * 8, LANES), F32),
            pltpu.VMEM((tiles * 8, LANES), F32),
            pltpu.VMEM((blocks, LANES), F32),
            pltpu.VMEM((table, LANES), jnp.int32),
            pltpu.SMEM((table, LANES), jnp.int32),
            pltpu.SemaphoreType.DMA((1 + len(mates),)),
            pltpu.SemaphoreType.DMA((1,)),
        ],
        name="pairs",
    )(own, *mates, *(() if first else (prev,)))


def exchange(own, size):
    def send(a, bit_of):
        return lax.ppermute(a, "space", [(i, i ^ bit_of(i)) for i in range(size)])

    def beside(i):
        return 1

    mate = send(own, beside)
    bits = [1 << k for k in range(1, size.bit_length() - 1)]
    if len(bits) == 2:
        def across(i):
            return bits[i % 2]

        far = send(own, across)
        far_mate = send(mate, across)
        far_beside = send(far, beside)
        corner = send(far_beside, across)
        return [[mate], [far, far_mate, far_beside, send(far_mate, beside)], [corner, send(corner, beside)]]
    held = [own, mate]
    for bit in bits:
        held.append(send(jnp.concatenate(held, 0), lambda i: bit))
    return [[mate], held[2:]]


def on_device(orbit_state, object_props, density_table, block_cube):
    next_state, own = propagate(density_table, orbit_state, object_props, block_cube)
    groups = exchange(own, lax.axis_size("space"))
    total = None
    for k, mates in enumerate(groups):
        total = pairs(own, mates, total, k == len(groups) - 1)
    return (next_state, total.reshape(orbit_state.shape[1]))


def solution(mesh):
    placed = (P(None, ("mc", "space")), P(None, ("mc", "space")), P(), P(("mc", "space")))
    return jax.shard_map(
        on_device,
        mesh=mesh,
        in_specs=placed,
        out_specs=(P(None, ("mc", "space")), P(("mc", "space"))),
        check_vma=False,
    )
```

```python
import functools

import jax
import jax.numpy as jnp
from jax import lax
from jax.experimental import pallas as pl
from jax.experimental.pallas import tpu as pltpu
from jax.sharding import PartitionSpec as P

LANES = 128
MOST = 4
SUB = 16
NTAB = 64

TIME_STEP = 0.2
EARTH_SPIN = 0.0588
J2_COEF = 0.00108263
DRAG_SCALE = 0.008
SCALE_HEIGHT = 0.1
TABLE_TOP = 0.4
SPEED_FLOOR = 0.04

F32 = jnp.float32
BF = jnp.bfloat16


def unit_rows(blocks):
    return 5 * blocks + -(-blocks // (8 * LANES)) * 8


def substep(state, ballistic, table, slopes):
    x, y, z, vx, vy, vz = state
    zz = z * z
    radius_sq = x * x + y * y + zz
    inv = lax.rsqrt(radius_sq)
    height = radius_sq * inv - 1.0
    coord = jnp.clip(height * ((NTAB - 1) / TABLE_TOP), -1.0, float(NTAB))
    cell = jnp.floor(coord)
    index = cell.astype(jnp.int32) + 1
    base = jnp.take_along_axis(table, index, axis=1, mode="promise_in_bounds")
    slope = jnp.take_along_axis(slopes, index, axis=1, mode="promise_in_bounds")
    log_density = base + (coord - cell) * slope - height * (1.0 / SCALE_HEIGHT)
    ux = vx + EARTH_SPIN * y
    uy = vy - EARTH_SPIN * x
    air_sq = ux * ux + uy * uy + vz * vz
    drag = (TIME_STEP * DRAG_SCALE) * jnp.exp(log_density) * (ballistic * jnp.sqrt(air_sq))
    inv_sq = inv * inv
    inv_cube = inv_sq * inv
    oblate = (1.5 * J2_COEF * TIME_STEP) * (inv_cube * inv_sq)
    pull = TIME_STEP * inv_cube + oblate * (1.0 - 5.0 * (zz * inv_sq))
    pull_z = pull + 2.0 * oblate
    vx = vx - x * pull - drag * ux
    vy = vy - y * pull - drag * uy
    vz = vz - z * pull_z - drag * vz
    return (x + TIME_STEP * vx, y + TIME_STEP * vy, z + TIME_STEP * vz, vx, vy, vz)


def propagate_kernel(table_ref, orbit_ref, props_ref, cube_ref, next_ref, unit_ref, tiles, props, lut, *, group, unroll):
    blocks = orbit_ref.shape[1] // LANES
    rows = group * 8
    for b in range(blocks):
        tiles[pl.ds(8 * b, 6), :] = orbit_ref[:, pl.ds(b * LANES, LANES)]
        props[pl.ds(8 * b, 3), :] = props_ref[:, pl.ds(b * LANES, LANES)]
    lut[...] = jnp.zeros((8, LANES), F32)
    lut[pl.ds(0, 1), pl.ds(0, NTAB)] = table_ref[...]
    knots = jnp.broadcast_to(lut[pl.ds(0, 1), :], (8, LANES))
    table = pltpu.roll(knots, 1, 1)
    slopes = jnp.tile(knots - table, (group, 1))
    table = jnp.tile(table, (group, 1))
    unit_ref[pl.ds(5 * blocks, unit_ref.shape[0] - 5 * blocks), :] = jnp.zeros(
        (unit_ref.shape[0] - 5 * blocks, LANES), F32
    )
    unit_ref[pl.ds(5 * blocks, blocks // LANES), :] = cube_ref[...].astype(F32)
    for i in range(blocks // rows):
        base = 8 * rows * i
        state = tuple(tiles[pl.ds(base + c, rows, stride=8), :] for c in range(6))
        radius, weight, ballistic = (props[pl.ds(base + c, rows, stride=8), :] for c in range(3))
        state = lax.fori_loop(
            0, SUB, lambda k, s: substep(s, ballistic, table, slopes), state, unroll=unroll
        )
        for c in range(6):
            tiles[pl.ds(base + c, rows, stride=8), :] = state[c]
        for c, plane in enumerate((*state[3:], radius, weight)):
            unit_ref[pl.ds(c * blocks + i * rows, rows), :] = plane
    for b in range(blocks):
        next_ref[:, pl.ds(b * LANES, LANES)] = tiles[pl.ds(8 * b, 6), :]


def propagate(density_table, orbit_state, object_props, block_cube):
    count = orbit_state.shape[1]
    blocks = count // LANES
    return pl.pallas_call(
        functools.partial(propagate_kernel, group=16, unroll=2),
        out_shape=(
            jax.ShapeDtypeStruct((6, count), F32),
            jax.ShapeDtypeStruct((unit_rows(blocks), LANES), F32),
        ),
        scratch_shapes=[
            pltpu.VMEM((blocks * 8, LANES), F32),
            pltpu.VMEM((blocks * 8, LANES), F32),
            pltpu.VMEM((8, LANES), F32),
        ],
        name="propagate",
    )(density_table.reshape(1, NTAB), orbit_state, object_props, block_cube.reshape(blocks // LANES, LANES))


def split(a):
    high = a.astype(BF).astype(F32)
    return jnp.concatenate([high, a - high], 0).astype(BF)


def whole_tiles(rows):
    extra = -len(rows) % 8
    return jnp.concatenate([*rows, *([jnp.zeros((extra, LANES), F32)] if extra else [])], 0)


def partner_table(own_ids, mate_ids, most, own_first):
    none = float(len(mate_ids) * LANES)
    sub = lax.broadcasted_iota(jnp.int32, (LANES, LANES), 0).astype(F32)
    lane = lax.broadcasted_iota(jnp.int32, (LANES, LANES), 1).astype(F32)
    cols = whole_tiles(mate_ids).T
    found = []
    for h, own in enumerate(own_ids):
        places = [
            jnp.where(cols[:, t : t + 1] == own, sub + float(t * LANES), none) for t in range(len(mate_ids))
        ]
        if own_first:
            places[h] = jnp.where(sub == lane, none, places[h])
        last = jnp.full((1, LANES), -1.0, F32)
        hits = []
        for _ in range(most):
            best = None
            for place in places:
                later = jnp.where(place > last, place, none)
                best = later if best is None else jnp.minimum(best, later)
            last = jnp.min(best, axis=0, keepdims=True)
            hits.append(last)
        found.append(hits)
    counts = [sum((hit < none).astype(F32) for hit in hits) for hits in found]
    rows = counts + [hit for hits in found for hit in hits]
    turned = whole_tiles(rows).T
    halves = len(own_ids)
    ordered = [[0.0] * (most + 2) for _ in range(halves)]
    for h in range(halves):
        count = turned[:, h : h + 1]
        ahead = 0.0
        for g in range(halves):
            before = (lane + float(g * LANES)) < (sub + float(h * LANES))
            ahead = ahead + jnp.where((counts[g] > count) | ((counts[g] == count) & before), 1.0, 0.0)
        rank = jnp.sum(ahead, axis=1, keepdims=True)
        for q in range(halves):
            here = rank == lane + float(q * LANES)
            take = lambda v: jnp.sum(jnp.where(here, v, 0.0), axis=0, keepdims=True)
            ordered[q][0] += take(sub + float(h * LANES))
            ordered[q][1] += take(count)
            for p in range(most):
                at = halves + h * most + p
                ordered[q][2 + p] += take(turned[:, at : at + 1])
    rows = [ordered[q][k] for k in range(most + 2) for q in range(halves)]
    return whole_tiles(rows).astype(jnp.int32)


def pairs_kernel(*refs, arrays, first, last, own_too, most, group):
    own_ref, *mate_refs = refs[: 1 + arrays]
    refs = refs[1 + arrays :]
    if not first:
        prev_ref, *refs = refs
    with_own = first or own_too
    out_ref, raw, ids_vmem, prev_vmem, own_tiles, mate_tiles, cols, table_vmem, table, sem, ids_sem, table_sem = refs
    blocks = out_ref.shape[0]
    rows = unit_rows(blocks)
    halves = blocks // LANES
    id_rows = rows - 5 * blocks
    copies, id_copies = [], []
    at = 0
    for k, ref in enumerate((own_ref, *mate_refs)):
        copies.append(pltpu.make_async_copy(ref, raw.at[pl.ds(at, ref.shape[0]), :], sem.at[k]))
        for r in range(0, ref.shape[0], rows):
            unit = (at + r) // rows
            src = ref.at[pl.ds(r + 5 * blocks, id_rows), :]
            dst = ids_vmem.at[pl.ds(unit * id_rows, id_rows), :]
            id_copies.append(pltpu.make_async_copy(src, dst, ids_sem.at[unit]))
        at += ref.shape[0]
    if not first:
        copies.append(pltpu.make_async_copy(prev_ref, prev_vmem, sem.at[1 + arrays]))
    for copy in id_copies + copies:
        copy.start()
    units = list(range(0 if with_own else 1, at // rows))
    cols[...] = jnp.zeros(cols.shape, F32)
    mate_tiles[pl.ds(len(units) * blocks * 8, 8), :] = jnp.zeros((8, LANES), F32)
    for copy in id_copies:
        copy.wait()
    if not first:

        def ids(unit):
            return [ids_vmem[pl.ds(unit * id_rows + h, 1), :] for h in range(halves)]

        table_vmem[...] = partner_table(ids(0), [row for u in units for row in ids(u)], most, own_too)
        to_smem = pltpu.make_async_copy(table_vmem, table, table_sem.at[0])
        to_smem.start()
    for copy in copies:
        copy.wait()
    one = jnp.ones((8, LANES), F32)

    def planes(unit, i):
        base = unit * rows + i * 8
        at = [pl.multiple_of(base + c * blocks, 8) for c in range(5)]
        return [raw[pl.ds(a, 8), :] for a in at]

    def own_tile(i, carry):
        vx, vy, vz, rad, _ = planes(0, i)
        speed_sq = vx * vx + vy * vy + vz * vz
        for k, row in enumerate((-2.0 * vx, -2.0 * vy, -2.0 * vz, one, speed_sq, rad * rad, 2.0 * rad, one)):
            own_tiles[pl.ds(i * 64 + k, 8, stride=8), :] = row
        return carry

    lax.fori_loop(0, blocks // 8, own_tile, 0, unroll=4)
    for n, unit in enumerate(units):

        def mate_tile(i, carry):
            vx, vy, vz, rad, wt = planes(unit, i)
            speed_sq = vx * vx + vy * vy + vz * vz + SPEED_FLOOR
            for k, row in enumerate((vx, vy, vz, speed_sq, one, wt, wt * rad, wt * rad * rad)):
                mate_tiles[pl.ds(n * blocks * 8 + i * 64 + k, 8, stride=8), :] = row
            return carry

        lax.fori_loop(0, blocks // 8, mate_tile, 0, unroll=4)
    if not first:
        to_smem.wait()
    lane = lax.broadcasted_iota(jnp.int32, (LANES, LANES), 1)
    is_gap = lax.broadcasted_iota(jnp.int32, (16, LANES), 0) % 8 < 5
    blank = jnp.zeros((16, LANES), BF)
    pad = jnp.zeros((96, LANES), BF)

    def run(q, place, count):
        for k in range(group):
            b = q * LANES + place + k if first else table[q, place + k]
            own = own_tiles[pl.ds(pl.multiple_of(b * 8, 8), 8), :]
            high = own.astype(BF).astype(F32)
            twice = [jnp.concatenate([part, part], 0).astype(BF) for part in (high, own - high)]
            lhs = jnp.concatenate([*twice, pad], 0).T
            acc = None
            for p in range(count):
                mate = b if first else table[(2 + p) * halves + q, place + k]
                parts = split(mate_tiles[pl.ds(pl.multiple_of(mate * 8, 8), 8), :])
                sides = []
                for side in (jnp.where(is_gap, parts, blank), jnp.where(is_gap, blank, parts)):
                    sides.append(jnp.concatenate([side, side, pad], 0))
                both = jnp.dot(lhs, jnp.concatenate(sides, 1), preferred_element_type=F32)
                gap = jnp.maximum(both[:, :LANES], SPEED_FLOOR)
                term = both[:, LANES:] * (gap * lax.rsqrt(gap))
                acc = term if acc is None else acc + term
            total = jnp.broadcast_to(jnp.sum(acc, axis=1, keepdims=True), (LANES, LANES))
            at = pl.multiple_of(jnp.bitwise_and(b, -LANES), LANES)
            pltpu.store(cols.at[pl.ds(at, LANES), :], total, mask=lane == jnp.bitwise_and(b, LANES - 1))

    def step(g, carry):
        q = g // (LANES // group)
        place = (g % (LANES // group)) * group
        if first:
            run(q, place, 1)
            return carry
        longest = table[halves + q, place]
        for count in range(1, most + 1):

            @pl.when(longest == count)
            def _():
                run(q, place, count)

        return carry

    lax.fori_loop(0, blocks // group, step, 0)
    for h in range(halves):
        at = pl.ds(h * LANES, LANES)
        total = cols[at, :].T
        rad = raw[pl.ds(3 * blocks + h * LANES, LANES), :]
        wt = raw[pl.ds(4 * blocks + h * LANES, LANES), :]
        if first:
            total = total - (4.0 * SPEED_FLOOR**0.5) * wt * rad * rad
        else:
            total = total + prev_vmem[at, :]
        if last:
            total = wt * total * (1.0 / (MOST * LANES))
        out_ref[at, :] = total


def pairs(own, mates, prev, own_too, last):
    rows = own.shape[0]
    blocks = rows // 5 // LANES * LANES
    first = prev is None
    most = MOST - 1
    total = sum(a.shape[0] for a in (own, *mates)) // rows
    tiles = (total if first or own_too else total - 1) * blocks + 1
    table = -(-(most + 2) * (blocks // LANES) // 8) * 8
    return pl.pallas_call(
        functools.partial(
            pairs_kernel, arrays=len(mates), first=first, last=last, own_too=own_too, most=most, group=64 if first else 32
        ),
        in_specs=[pl.BlockSpec(memory_space=pl.ANY)] * (len(mates) + (1 if first else 2)),
        out_shape=jax.ShapeDtypeStruct((blocks, LANES), F32),
        scratch_shapes=[
            pltpu.VMEM((total * rows, LANES), F32),
            pltpu.VMEM((total * (rows - 5 * blocks), LANES), F32),
            pltpu.VMEM((blocks, LANES), F32),
            pltpu.VMEM((blocks * 8, LANES), F32),
            pltpu.VMEM((tiles * 8, LANES), F32),
            pltpu.VMEM((blocks, LANES), F32),
            pltpu.VMEM((table, LANES), jnp.int32),
            pltpu.SMEM((table, LANES), jnp.int32),
            pltpu.SemaphoreType.DMA((2 + len(mates),)),
            pltpu.SemaphoreType.DMA((total,)),
            pltpu.SemaphoreType.DMA((1,)),
        ],
        name="pairs",
    )(own, *mates, *(() if first else (prev,)))


def exchange(own, size):
    def send(a, bit_of):
        return lax.ppermute(a, "space", [(i, i ^ bit_of(i)) for i in range(size)])

    def beside(i):
        return 1

    mate = send(own, beside)
    bits = [1 << k for k in range(1, size.bit_length() - 1)]
    if len(bits) == 2:
        def across(i):
            return bits[i % 2]

        far = send(own, across)
        far_mate = send(mate, across)
        far_beside = send(far, beside)
        corner = send(far_beside, across)
        far_mate_beside = send(far_mate, beside)
        corner_beside = send(corner, beside)
        return [[mate, far, far_beside], [far_mate, far_mate_beside, corner, corner_beside]]
    held = [own, mate]
    for bit in bits:
        held.append(send(jnp.concatenate(held, 0), lambda i: bit))
    return [[mate], held[2:]]


def on_device(orbit_state, object_props, density_table, block_cube):
    next_state, own = propagate(density_table, orbit_state, object_props, block_cube)
    groups = exchange(own, lax.axis_size("space"))
    total = pairs(own, [], None, False, False)
    for k, mates in enumerate(groups):
        total = pairs(own, mates, total, k == 0, k == len(groups) - 1)
    return (next_state, total.reshape(orbit_state.shape[1]))


def solution(mesh):
    placed = (P(None, ("mc", "space")), P(None, ("mc", "space")), P(), P(("mc", "space")))
    return jax.shard_map(
        on_device,
        mesh=mesh,
        in_specs=placed,
        out_specs=(P(None, ("mc", "space")), P(("mc", "space"))),
        check_vma=False,
    )
```

```python
import functools
import math

import jax
import jax.numpy as jnp
from jax import lax
from jax.experimental import pallas as pl
from jax.experimental.pallas import tpu as pltpu
from jax.sharding import PartitionSpec as P

LANES = 128
MOST = 4
SUB = 16
NTAB = 64

TIME_STEP = 0.2
EARTH_SPIN = 0.0588
J2_COEF = 0.00108263
DRAG_SCALE = 0.008
SCALE_HEIGHT = 0.1
TABLE_TOP = 0.4
SPEED_FLOOR = 0.04
TINY = 1e-30
KEPT_VMEM = 8 << 20
KERNEL_VMEM = 32 << 20
LOG2_E = math.log2(math.e)

F32 = jnp.float32
BF = jnp.bfloat16


def unit_rows(blocks):
    return 5 * blocks + -(-blocks // (8 * LANES)) * 8


def lookup(table, index):
    dims = lax.GatherDimensionNumbers(
        offset_dims=(),
        collapsed_slice_dims=(1,),
        start_index_map=(1,),
        operand_batching_dims=(0,),
        start_indices_batching_dims=(0,),
    )
    mode = lax.GatherScatterMode.PROMISE_IN_BOUNDS
    return lax.gather(table, index[:, :, None], dims, (1, 1), mode=mode)


def substep(state, ballistic, table, slopes):
    x, y, z, dx, dy, dz = state
    zz = z * z
    radius_sq = x * x + y * y + zz
    inv = lax.rsqrt(radius_sq)
    radius = radius_sq * inv
    cells = (NTAB - 1) / TABLE_TOP
    coord = jnp.clip(radius * cells + (1.0 - cells), 0.0, NTAB + 1.0)
    index = coord.astype(jnp.int32)
    fraction = coord - index.astype(F32)
    fall = LOG2_E / SCALE_HEIGHT
    log_density = radius * -fall + (fall + math.log2(DRAG_SCALE))
    log_density = log_density + (lookup(table, index) + fraction * lookup(slopes, index))
    ux = dx + (TIME_STEP * EARTH_SPIN) * y
    uy = dy - (TIME_STEP * EARTH_SPIN) * x
    air_sq = ux * ux + uy * uy + dz * dz
    drag = jnp.exp2(log_density) * (ballistic * (air_sq * lax.rsqrt(jnp.maximum(air_sq, TINY))))
    inv_sq = inv * inv
    oblate = (1.5 * J2_COEF * TIME_STEP**2) * inv_sq
    base = TIME_STEP**2 - (5.0 * oblate) * (zz * inv_sq)
    inv_cube = inv_sq * inv
    pull = inv_cube * (base + oblate)
    pull_z = inv_cube * (base + 3.0 * oblate)
    dx = dx - x * pull - drag * ux
    dy = dy - y * pull - drag * uy
    dz = dz - z * pull_z - drag * dz
    return (x + dx, y + dy, z + dz, dx, dy, dz)


def propagate_kernel(table_ref, orbit_ref, props_ref, cube_ref, next_ref, unit_ref, tiles, props, lut, *, group, unroll):
    blocks = orbit_ref.shape[1] // LANES
    rows = group * 8
    for b in range(blocks):
        tiles[pl.ds(8 * b, 6), :] = orbit_ref[:, pl.ds(b * LANES, LANES)]
        props[pl.ds(8 * b, 3), :] = props_ref[:, pl.ds(b * LANES, LANES)]
    lut[...] = jnp.zeros((8, LANES), F32)
    lut[pl.ds(0, 1), pl.ds(0, NTAB)] = table_ref[...] * LOG2_E
    knots = jnp.broadcast_to(lut[pl.ds(0, 1), :], (8, LANES))
    table = pltpu.roll(knots, 1, 1)
    slopes = jnp.tile(knots - table, (group, 1))
    table = jnp.tile(table, (group, 1))
    unit_ref[pl.ds(5 * blocks, unit_ref.shape[0] - 5 * blocks), :] = jnp.zeros(
        (unit_ref.shape[0] - 5 * blocks, LANES), F32
    )
    unit_ref[pl.ds(5 * blocks, blocks // LANES), :] = cube_ref[...].astype(F32)
    for i in range(blocks // rows):
        base = 8 * rows * i
        state = [tiles[pl.ds(base + c, rows, stride=8), :] for c in range(6)]
        state = (*state[:3], *(TIME_STEP * v for v in state[3:]))
        radius, weight, ballistic = (props[pl.ds(base + c, rows, stride=8), :] for c in range(3))
        state = lax.fori_loop(
            0, SUB, lambda k, s: substep(s, ballistic, table, slopes), state, unroll=unroll
        )
        state = (*state[:3], *((1.0 / TIME_STEP) * d for d in state[3:]))
        for c in range(6):
            tiles[pl.ds(base + c, rows, stride=8), :] = state[c]
        for c, plane in enumerate((*state[3:], radius, weight)):
            unit_ref[pl.ds(c * blocks + i * rows, rows), :] = plane
    for b in range(blocks):
        next_ref[:, pl.ds(b * LANES, LANES)] = tiles[pl.ds(8 * b, 6), :]


def propagate(density_table, orbit_state, object_props, block_cube):
    count = orbit_state.shape[1]
    blocks = count // LANES
    return pl.pallas_call(
        functools.partial(propagate_kernel, group=16, unroll=2),
        out_shape=(
            jax.ShapeDtypeStruct((6, count), F32),
            jax.ShapeDtypeStruct((unit_rows(blocks), LANES), F32),
        ),
        scratch_shapes=[
            pltpu.VMEM((blocks * 8, LANES), F32),
            pltpu.VMEM((blocks * 8, LANES), F32),
            pltpu.VMEM((8, LANES), F32),
        ],
        name="propagate",
    )(density_table.reshape(1, NTAB), orbit_state, object_props, block_cube.reshape(blocks // LANES, LANES))


def split(a):
    high = a.astype(BF).astype(F32)
    return jnp.concatenate([high, a - high], 0).astype(BF)


def whole_tiles(rows):
    extra = -len(rows) % 8
    return jnp.concatenate([*rows, *([jnp.zeros((extra, LANES), F32)] if extra else [])], 0)


def partner_table(own_ids, mate_ids, most, own_first):
    none = float(len(mate_ids) * LANES)
    sub = lax.broadcasted_iota(jnp.int32, (LANES, LANES), 0).astype(F32)
    lane = lax.broadcasted_iota(jnp.int32, (LANES, LANES), 1).astype(F32)
    cols = whole_tiles(mate_ids).T
    found = []
    for h, own in enumerate(own_ids):
        places = [
            jnp.where(cols[:, t : t + 1] == own, sub + float(t * LANES), none) for t in range(len(mate_ids))
        ]
        if own_first:
            places[h] = jnp.where(sub == lane, none, places[h])
        last = jnp.full((1, LANES), -1.0, F32)
        hits = []
        for _ in range(most):
            best = None
            for place in places:
                later = jnp.where(place > last, place, none)
                best = later if best is None else jnp.minimum(best, later)
            last = jnp.min(best, axis=0, keepdims=True)
            hits.append(last)
        found.append(hits)
    counts = [sum((hit < none).astype(F32) for hit in hits) for hits in found]
    rows = counts + [hit for hits in found for hit in hits]
    turned = whole_tiles(rows).T
    halves = len(own_ids)
    ordered = [[0.0] * (most + 2) for _ in range(halves)]
    for h in range(halves):
        count = turned[:, h : h + 1]
        ahead = 0.0
        for g in range(halves):
            before = (lane + float(g * LANES)) < (sub + float(h * LANES))
            ahead = ahead + jnp.where((counts[g] > count) | ((counts[g] == count) & before), 1.0, 0.0)
        rank = jnp.sum(ahead, axis=1, keepdims=True)
        for q in range(halves):
            here = rank == lane + float(q * LANES)
            take = lambda v: jnp.sum(jnp.where(here, v, 0.0), axis=0, keepdims=True)
            ordered[q][0] += take(sub + float(h * LANES))
            ordered[q][1] += take(count)
            for p in range(most):
                at = halves + h * most + p
                ordered[q][2 + p] += take(turned[:, at : at + 1])
    rows = [ordered[q][k] for k in range(most + 2) for q in range(halves)]
    return whole_tiles(rows).astype(jnp.int32)


def pairs_kernel(*refs, arrays, first, last, own_too, most, group):
    own_ref, *mate_refs = refs[: 1 + arrays]
    refs = refs[1 + arrays :]
    if not first:
        prev_ref, *refs = refs
    with_own = first or own_too
    out_ref, own_tiles, mate_tiles, cols, table_vmem, table, table_sem = refs
    blocks = out_ref.shape[0]
    rows = unit_rows(blocks)
    halves = blocks // LANES
    units = [(ref, r) for ref in ((own_ref,) if with_own else ()) + tuple(mate_refs) for r in range(0, ref.shape[0], rows)]
    if not first:

        def ids(unit):
            ref, at = unit
            return [ref[pl.ds(at + 5 * blocks + h, 1), :] for h in range(halves)]

        table_vmem[...] = partner_table(ids((own_ref, 0)), [row for u in units for row in ids(u)], most, own_too)
        to_smem = pltpu.make_async_copy(table_vmem, table, table_sem.at[0])
        to_smem.start()
    cols[...] = jnp.zeros(cols.shape, F32)
    mate_tiles[pl.ds(len(units) * blocks * 8, 8), :] = jnp.zeros((8, LANES), F32)
    one = jnp.ones((8, LANES), F32)

    def planes(unit, i):
        ref, base = unit
        at = [pl.multiple_of(base + c * blocks + i * 8, 8) for c in range(5)]
        return [ref[pl.ds(a, 8), :] for a in at]

    def own_tile(i, carry):
        vx, vy, vz, rad, _ = planes((own_ref, 0), i)
        speed_sq = vx * vx + vy * vy + vz * vz
        for k, row in enumerate((-2.0 * vx, -2.0 * vy, -2.0 * vz, one, speed_sq, rad * rad, 2.0 * rad, one)):
            own_tiles[pl.ds(i * 64 + k, 8, stride=8), :] = row
        return carry

    lax.fori_loop(0, blocks // 8, own_tile, 0, unroll=4)
    for n, unit in enumerate(units):

        def mate_tile(i, carry):
            vx, vy, vz, rad, wt = planes(unit, i)
            speed_sq = vx * vx + vy * vy + vz * vz + SPEED_FLOOR
            for k, row in enumerate((vx, vy, vz, speed_sq, one, wt, wt * rad, wt * rad * rad)):
                mate_tiles[pl.ds(n * blocks * 8 + i * 64 + k, 8, stride=8), :] = row
            return carry

        lax.fori_loop(0, blocks // 8, mate_tile, 0, unroll=4)
    if not first:
        to_smem.wait()
    lane = lax.broadcasted_iota(jnp.int32, (LANES, LANES), 1)
    is_gap = lax.broadcasted_iota(jnp.int32, (16, LANES), 0) % 8 < 5
    blank = jnp.zeros((16, LANES), BF)
    pad = jnp.zeros((96, LANES), BF)

    def run(q, place, count):
        for k in range(group):
            b = q * LANES + place + k if first else table[q, place + k]
            own = own_tiles[pl.ds(pl.multiple_of(b * 8, 8), 8), :]
            high = own.astype(BF).astype(F32)
            twice = [jnp.concatenate([part, part], 0).astype(BF) for part in (high, own - high)]
            lhs = jnp.concatenate([*twice, pad], 0).T
            acc = None
            for p in range(count):
                mate = b if first else table[(2 + p) * halves + q, place + k]
                parts = split(mate_tiles[pl.ds(pl.multiple_of(mate * 8, 8), 8), :])
                sides = []
                for side in (jnp.where(is_gap, parts, blank), jnp.where(is_gap, blank, parts)):
                    sides.append(jnp.concatenate([side, side, pad], 0))
                both = jnp.dot(lhs, jnp.concatenate(sides, 1), preferred_element_type=F32)
                gap = jnp.maximum(both[:, :LANES], SPEED_FLOOR)
                term = both[:, LANES:] * (gap * lax.rsqrt(gap))
                acc = term if acc is None else acc + term
            total = jnp.broadcast_to(jnp.sum(acc, axis=1, keepdims=True), (LANES, LANES))
            at = pl.multiple_of(jnp.bitwise_and(b, -LANES), LANES)
            pltpu.store(cols.at[pl.ds(at, LANES), :], total, mask=lane == jnp.bitwise_and(b, LANES - 1))

    def step(g, carry):
        q = g // (LANES // group)
        place = (g % (LANES // group)) * group
        if first:
            run(q, place, 1)
            return carry
        longest = table[halves + q, place]
        for count in range(1, most + 1):

            @pl.when(longest == count)
            def _():
                run(q, place, count)

        return carry

    lax.fori_loop(0, blocks // group, step, 0)
    for h in range(halves):
        at = pl.ds(h * LANES, LANES)
        total = cols[at, :].T
        rad = own_ref[pl.ds(3 * blocks + h * LANES, LANES), :]
        wt = own_ref[pl.ds(4 * blocks + h * LANES, LANES), :]
        if first:
            total = total - (4.0 * SPEED_FLOOR**0.5) * wt * rad * rad
        else:
            total = total + prev_ref[at, :]
        if last:
            total = wt * total * (1.0 / (MOST * LANES))
        out_ref[at, :] = total


def pairs(own, mates, prev, own_too, last, resident):
    rows = own.shape[0]
    blocks = rows // 5 // LANES * LANES
    first = prev is None
    most = MOST - 1
    units = sum(a.shape[0] for a in mates) // rows + (1 if first or own_too else 0)
    table = -(-(most + 2) * (blocks // LANES) // 8) * 8
    operands = [own, *mates, *(() if first else (prev,))]
    if resident:
        operands = [pltpu.with_memory_space_constraint(a, pltpu.VMEM) for a in operands]
    return pl.pallas_call(
        functools.partial(
            pairs_kernel,
            arrays=len(mates),
            first=first,
            last=last,
            own_too=own_too,
            most=most,
            group=64 if first else 32,
        ),
        in_specs=[pl.BlockSpec(memory_space=pltpu.VMEM)] * len(operands),
        out_shape=jax.ShapeDtypeStruct((blocks, LANES), F32),
        scratch_shapes=[
            pltpu.VMEM((blocks * 8, LANES), F32),
            pltpu.VMEM(((units * blocks + 1) * 8, LANES), F32),
            pltpu.VMEM((blocks, LANES), F32),
            pltpu.VMEM((table, LANES), jnp.int32),
            pltpu.SMEM((table, LANES), jnp.int32),
            pltpu.SemaphoreType.DMA((1,)),
        ],
        compiler_params=pltpu.CompilerParams(vmem_limit_bytes=KERNEL_VMEM) if resident else None,
        name="pairs",
    )(*operands)


def exchange(own, size):
    def send(a, bit_of):
        return lax.ppermute(a, "space", [(i, i ^ bit_of(i)) for i in range(size)])

    def beside(i):
        return 1

    mate = send(own, beside)
    bits = [1 << k for k in range(1, size.bit_length() - 1)]
    if len(bits) == 2:
        def across(i):
            return bits[i % 2]

        far = send(own, across)
        far_mate = send(mate, across)
        far_beside = send(far, beside)
        corner = send(far_beside, across)
        far_mate_beside = send(far_mate, beside)
        corner_beside = send(corner, beside)
        return [[mate, far, far_beside], [far_mate, far_mate_beside, corner, corner_beside]]
    held = [own, mate]
    for bit in bits:
        held.append(send(jnp.concatenate(held, 0), lambda i: bit))
    return [[mate], held[2:]]


def on_device(orbit_state, object_props, density_table, block_cube):
    next_state, own = propagate(density_table, orbit_state, object_props, block_cube)
    groups = exchange(own, lax.axis_size("space"))
    resident = sum(a.size for mates in groups for a in mates) * 4 <= KEPT_VMEM
    total = pairs(own, [], None, False, False, resident)
    for k, mates in enumerate(groups):
        total = pairs(own, mates, total, k == 0, k == len(groups) - 1, resident)
    return (next_state, total.reshape(orbit_state.shape[1]))


def solution(mesh):
    placed = (P(None, ("mc", "space")), P(None, ("mc", "space")), P(), P(("mc", "space")))
    return jax.shard_map(
        on_device,
        mesh=mesh,
        in_specs=placed,
        out_specs=(P(None, ("mc", "space")), P(("mc", "space"))),
        check_vma=False,
    )
```

```python
import functools
import math

import jax
import jax.numpy as jnp
from jax import lax
from jax.experimental import pallas as pl
from jax.experimental.pallas import tpu as pltpu
from jax.sharding import PartitionSpec as P

LANES = 128
MOST = 4
SUB = 16
NTAB = 64

TIME_STEP = 0.2
EARTH_SPIN = 0.0588
J2_COEF = 0.00108263
DRAG_SCALE = 0.008
SCALE_HEIGHT = 0.1
TABLE_TOP = 0.4
SPEED_FLOOR = 0.04
TINY = 1e-30
KEPT_VMEM = 8 << 20
KERNEL_VMEM = 32 << 20
LOG2_E = math.log2(math.e)

F32 = jnp.float32
BF = jnp.bfloat16


def unit_rows(blocks):
    return 5 * blocks + -(-blocks // (8 * LANES)) * 8


def lookup(table, index):
    dims = lax.GatherDimensionNumbers(
        offset_dims=(),
        collapsed_slice_dims=(1,),
        start_index_map=(1,),
        operand_batching_dims=(0,),
        start_indices_batching_dims=(0,),
    )
    mode = lax.GatherScatterMode.PROMISE_IN_BOUNDS
    return lax.gather(table, index[:, :, None], dims, (1, 1), mode=mode)


def substep(state, ballistic, table, slopes):
    x, y, z, dx, dy, dz = state
    zz = z * z
    radius_sq = x * x + y * y + zz
    inv = lax.rsqrt(radius_sq)
    radius = radius_sq * inv
    cells = (NTAB - 1) / TABLE_TOP
    coord = jnp.clip(radius * cells + (1.0 - cells), 0.0, NTAB + 1.0)
    index = coord.astype(jnp.int32)
    fraction = coord - index.astype(F32)
    fall = LOG2_E / SCALE_HEIGHT
    log_density = radius * -fall + (fall + math.log2(DRAG_SCALE))
    log_density = log_density + (lookup(table, index) + fraction * lookup(slopes, index))
    ux = dx + (TIME_STEP * EARTH_SPIN) * y
    uy = dy - (TIME_STEP * EARTH_SPIN) * x
    air_sq = ux * ux + uy * uy + dz * dz
    drag = jnp.exp2(log_density) * (ballistic * (air_sq * lax.rsqrt(jnp.maximum(air_sq, TINY))))
    inv_sq = inv * inv
    oblate = (1.5 * J2_COEF * TIME_STEP**2) * inv_sq
    base = TIME_STEP**2 - (5.0 * oblate) * (zz * inv_sq)
    inv_cube = inv_sq * inv
    pull = inv_cube * (base + oblate)
    pull_z = inv_cube * (base + 3.0 * oblate)
    dx = dx - x * pull - drag * ux
    dy = dy - y * pull - drag * uy
    dz = dz - z * pull_z - drag * dz
    return (x + dx, y + dy, z + dz, dx, dy, dz)


def propagate_kernel(table_ref, orbit_ref, props_ref, cube_ref, next_ref, unit_ref, tiles, props, lut, *, group, unroll):
    blocks = orbit_ref.shape[1] // LANES
    rows = group * 8
    for b in range(blocks):
        tiles[pl.ds(8 * b, 6), :] = orbit_ref[:, pl.ds(b * LANES, LANES)]
        props[pl.ds(8 * b, 3), :] = props_ref[:, pl.ds(b * LANES, LANES)]
    lut[...] = jnp.zeros((8, LANES), F32)
    lut[pl.ds(0, 1), pl.ds(0, NTAB)] = table_ref[...] * LOG2_E
    knots = jnp.broadcast_to(lut[pl.ds(0, 1), :], (8, LANES))
    table = pltpu.roll(knots, 1, 1)
    slopes = jnp.tile(knots - table, (group, 1))
    table = jnp.tile(table, (group, 1))
    unit_ref[pl.ds(5 * blocks, unit_ref.shape[0] - 5 * blocks), :] = jnp.zeros(
        (unit_ref.shape[0] - 5 * blocks, LANES), F32
    )
    unit_ref[pl.ds(5 * blocks, blocks // LANES), :] = cube_ref[...].astype(F32)
    for i in range(blocks // rows):
        base = 8 * rows * i
        state = [tiles[pl.ds(base + c, rows, stride=8), :] for c in range(6)]
        state = (*state[:3], *(TIME_STEP * v for v in state[3:]))
        radius, weight, ballistic = (props[pl.ds(base + c, rows, stride=8), :] for c in range(3))
        state = lax.fori_loop(
            0, SUB, lambda k, s: substep(s, ballistic, table, slopes), state, unroll=unroll
        )
        state = (*state[:3], *((1.0 / TIME_STEP) * d for d in state[3:]))
        for c in range(6):
            tiles[pl.ds(base + c, rows, stride=8), :] = state[c]
        for c, plane in enumerate((*state[3:], radius, weight)):
            unit_ref[pl.ds(c * blocks + i * rows, rows), :] = plane
    for b in range(blocks):
        next_ref[:, pl.ds(b * LANES, LANES)] = tiles[pl.ds(8 * b, 6), :]


def result(shape, dtype, resident):
    return pltpu.VMEM(shape, dtype) if resident else jax.ShapeDtypeStruct(shape, dtype)


def propagate(density_table, orbit_state, object_props, block_cube, resident):
    count = orbit_state.shape[1]
    blocks = count // LANES
    return pl.pallas_call(
        functools.partial(propagate_kernel, group=16, unroll=2),
        out_shape=(
            jax.ShapeDtypeStruct((6, count), F32),
            result((unit_rows(blocks), LANES), F32, resident),
        ),
        scratch_shapes=[
            pltpu.VMEM((blocks * 8, LANES), F32),
            pltpu.VMEM((blocks * 8, LANES), F32),
            pltpu.VMEM((8, LANES), F32),
        ],
        compiler_params=pltpu.CompilerParams(vmem_limit_bytes=KERNEL_VMEM) if resident else None,
        name="propagate",
    )(density_table.reshape(1, NTAB), orbit_state, object_props, block_cube.reshape(blocks // LANES, LANES))


def split(a):
    high = a.astype(BF).astype(F32)
    return jnp.concatenate([high, a - high], 0).astype(BF)


def whole_tiles(rows):
    extra = -len(rows) % 8
    return jnp.concatenate([*rows, *([jnp.zeros((extra, LANES), F32)] if extra else [])], 0)


def partner_table(own_ids, mate_ids, most, own_first):
    none = float(len(mate_ids) * LANES)
    sub = lax.broadcasted_iota(jnp.int32, (LANES, LANES), 0).astype(F32)
    lane = lax.broadcasted_iota(jnp.int32, (LANES, LANES), 1).astype(F32)
    cols = whole_tiles(mate_ids).T
    found = []
    for h, own in enumerate(own_ids):
        places = [
            jnp.where(cols[:, t : t + 1] == own, sub + float(t * LANES), none) for t in range(len(mate_ids))
        ]
        if own_first:
            places[h] = jnp.where(sub == lane, none, places[h])
        last = jnp.full((1, LANES), -1.0, F32)
        hits = []
        for _ in range(most):
            best = None
            for place in places:
                later = jnp.where(place > last, place, none)
                best = later if best is None else jnp.minimum(best, later)
            last = jnp.min(best, axis=0, keepdims=True)
            hits.append(last)
        found.append(hits)
    counts = [sum((hit < none).astype(F32) for hit in hits) for hits in found]
    rows = counts + [hit for hits in found for hit in hits]
    turned = whole_tiles(rows).T
    halves = len(own_ids)
    ordered = [[0.0] * (most + 2) for _ in range(halves)]
    for h in range(halves):
        count = turned[:, h : h + 1]
        ahead = 0.0
        for g in range(halves):
            before = (lane + float(g * LANES)) < (sub + float(h * LANES))
            ahead = ahead + jnp.where((counts[g] > count) | ((counts[g] == count) & before), 1.0, 0.0)
        rank = jnp.sum(ahead, axis=1, keepdims=True)
        for q in range(halves):
            here = rank == lane + float(q * LANES)
            take = lambda v: jnp.sum(jnp.where(here, v, 0.0), axis=0, keepdims=True)
            ordered[q][0] += take(sub + float(h * LANES))
            ordered[q][1] += take(count)
            for p in range(most):
                at = halves + h * most + p
                ordered[q][2 + p] += take(turned[:, at : at + 1])
    rows = [ordered[q][k] for k in range(most + 2) for q in range(halves)]
    return whole_tiles(rows).astype(jnp.int32)


def pairs_kernel(*refs, arrays, first, last, own_too, most, group):
    own_ref, *mate_refs = refs[: 1 + arrays]
    refs = refs[1 + arrays :]
    if first:
        out_ref, lhs_ref, *refs = refs
    else:
        prev_ref, lhs_ref, out_ref, *refs = refs
    with_own = first or own_too
    own_tiles, mate_tiles, cols, table_vmem, table, table_sem = refs
    blocks = out_ref.shape[0]
    rows = unit_rows(blocks)
    halves = blocks // LANES
    units = [(ref, r) for ref in ((own_ref,) if with_own else ()) + tuple(mate_refs) for r in range(0, ref.shape[0], rows)]
    if not first:

        def ids(unit):
            ref, at = unit
            return [ref[pl.ds(at + 5 * blocks + h, 1), :] for h in range(halves)]

        table_vmem[...] = partner_table(ids((own_ref, 0)), [row for u in units for row in ids(u)], most, own_too)
        to_smem = pltpu.make_async_copy(table_vmem, table, table_sem.at[0])
        to_smem.start()
    cols[...] = jnp.zeros(cols.shape, F32)
    mate_tiles[pl.ds(len(units) * blocks * 8, 8), :] = jnp.zeros((8, LANES), F32)
    one = jnp.ones((8, LANES), F32)

    def planes(unit, i):
        ref, base = unit
        at = [pl.multiple_of(base + c * blocks + i * 8, 8) for c in range(5)]
        return [ref[pl.ds(a, 8), :] for a in at]

    def own_tile(i, carry):
        vx, vy, vz, rad, _ = planes((own_ref, 0), i)
        speed_sq = vx * vx + vy * vy + vz * vz
        for k, row in enumerate((-2.0 * vx, -2.0 * vy, -2.0 * vz, one, speed_sq, rad * rad, 2.0 * rad, one)):
            own_tiles[pl.ds(i * 64 + k, 8, stride=8), :] = row
        return carry

    if first:
        lax.fori_loop(0, blocks // 8, own_tile, 0, unroll=4)
    for n, unit in enumerate(units):

        def mate_tile(i, carry):
            vx, vy, vz, rad, wt = planes(unit, i)
            speed_sq = vx * vx + vy * vy + vz * vz + SPEED_FLOOR
            for k, row in enumerate((vx, vy, vz, speed_sq, one, wt, wt * rad, wt * rad * rad)):
                mate_tiles[pl.ds(n * blocks * 8 + i * 64 + k, 8, stride=8), :] = row
            return carry

        lax.fori_loop(0, blocks // 8, mate_tile, 0, unroll=4)
    if not first:
        to_smem.wait()
    lane = lax.broadcasted_iota(jnp.int32, (LANES, LANES), 1)
    is_gap = lax.broadcasted_iota(jnp.int32, (16, LANES), 0) % 8 < 5
    blank = jnp.zeros((16, LANES), BF)
    pad = jnp.zeros((96, LANES), BF)

    def run(q, place, count):
        for k in range(group):
            b = q * LANES + place + k if first else table[q, place + k]
            features = pl.ds(pl.multiple_of(b * LANES, LANES), LANES)
            if first:
                own = own_tiles[pl.ds(pl.multiple_of(b * 8, 8), 8), :]
                high = own.astype(BF).astype(F32)
                twice = [jnp.concatenate([part, part], 0).astype(BF) for part in (high, own - high)]
                lhs = jnp.concatenate([*twice, pad], 0).T
                lhs_ref[features, :] = lhs
            else:
                lhs = lhs_ref[features, :]
            acc = None
            for p in range(count):
                mate = b if first else table[(2 + p) * halves + q, place + k]
                parts = split(mate_tiles[pl.ds(pl.multiple_of(mate * 8, 8), 8), :])
                sides = []
                for side in (jnp.where(is_gap, parts, blank), jnp.where(is_gap, blank, parts)):
                    sides.append(jnp.concatenate([side, side, pad], 0))
                both = jnp.dot(lhs, jnp.concatenate(sides, 1), preferred_element_type=F32)
                gap = jnp.maximum(both[:, :LANES], SPEED_FLOOR)
                term = both[:, LANES:] * (gap * lax.rsqrt(gap))
                acc = term if acc is None else acc + term
            total = jnp.broadcast_to(jnp.sum(acc, axis=1, keepdims=True), (LANES, LANES))
            at = pl.multiple_of(jnp.bitwise_and(b, -LANES), LANES)
            pltpu.store(cols.at[pl.ds(at, LANES), :], total, mask=lane == jnp.bitwise_and(b, LANES - 1))

    def step(g, carry):
        q = g // (LANES // group)
        place = (g % (LANES // group)) * group
        if first:
            run(q, place, 1)
            return carry
        longest = table[halves + q, place]
        for count in range(1, most + 1):

            @pl.when(longest == count)
            def _():
                run(q, place, count)

        return carry

    lax.fori_loop(0, blocks // group, step, 0)
    for h in range(halves):
        at = pl.ds(h * LANES, LANES)
        total = cols[at, :].T
        rad = own_ref[pl.ds(3 * blocks + h * LANES, LANES), :]
        wt = own_ref[pl.ds(4 * blocks + h * LANES, LANES), :]
        if first:
            total = total - (4.0 * SPEED_FLOOR**0.5) * wt * rad * rad
        else:
            total = total + prev_ref[at, :]
        if last:
            total = wt * total * (1.0 / (MOST * LANES))
        out_ref[at, :] = total


def pairs(own, mates, prev, lhs, own_too, last, resident):
    rows = own.shape[0]
    blocks = rows // 5 // LANES * LANES
    first = prev is None
    most = MOST - 1
    units = sum(a.shape[0] for a in mates) // rows + (1 if first or own_too else 0)
    table = -(-(most + 2) * (blocks // LANES) // 8) * 8
    operands = [own, *mates, *(() if first else (prev, lhs))]
    total = result((blocks, LANES), F32, resident and not last)
    if resident:
        operands = [pltpu.with_memory_space_constraint(a, pltpu.VMEM) for a in operands]
    return pl.pallas_call(
        functools.partial(
            pairs_kernel,
            arrays=len(mates),
            first=first,
            last=last,
            own_too=own_too,
            most=most,
            group=64 if first else 32,
        ),
        in_specs=[pl.BlockSpec(memory_space=pltpu.VMEM)] * len(operands),
        out_shape=(total, result((blocks * LANES, LANES), BF, resident)) if first else total,
        scratch_shapes=[
            pltpu.VMEM((blocks * 8, LANES), F32),
            pltpu.VMEM(((units * blocks + 1) * 8, LANES), F32),
            pltpu.VMEM((blocks, LANES), F32),
            pltpu.VMEM((table, LANES), jnp.int32),
            pltpu.SMEM((table, LANES), jnp.int32),
            pltpu.SemaphoreType.DMA((1,)),
        ],
        compiler_params=pltpu.CompilerParams(vmem_limit_bytes=KERNEL_VMEM) if resident else None,
        name="pairs",
    )(*operands)


def exchange(own, size):
    def send(a, bit_of):
        return lax.ppermute(a, "space", [(i, i ^ bit_of(i)) for i in range(size)])

    def beside(i):
        return 1

    mate = send(own, beside)
    bits = [1 << k for k in range(1, size.bit_length() - 1)]
    if len(bits) == 2:
        def across(i):
            return bits[i % 2]

        far = send(own, across)
        far_mate = send(mate, across)
        far_beside = send(far, beside)
        corner = send(far_beside, across)
        far_mate_beside = send(far_mate, beside)
        corner_beside = send(corner, beside)
        return [[mate, far, far_beside], [far_mate, far_mate_beside, corner, corner_beside]]
    held = [own, mate]
    for bit in bits:
        held.append(send(jnp.concatenate(held, 0), lambda i: bit))
    return [[mate], held[2:]]


def on_device(orbit_state, object_props, density_table, block_cube):
    size = lax.axis_size("space")
    blocks = block_cube.shape[0]
    resident = size * unit_rows(blocks) * LANES * 4 <= KEPT_VMEM
    next_state, own = propagate(density_table, orbit_state, object_props, block_cube, resident)
    groups = exchange(own, size)
    total, lhs = pairs(own, [], None, None, False, False, resident)
    for k, mates in enumerate(groups):
        total = pairs(own, mates, total, lhs, k == 0, k == len(groups) - 1, resident)
    return (next_state, total.reshape(orbit_state.shape[1]))


def solution(mesh):
    placed = (P(None, ("mc", "space")), P(None, ("mc", "space")), P(), P(("mc", "space")))
    return jax.shard_map(
        on_device,
        mesh=mesh,
        in_specs=placed,
        out_specs=(P(None, ("mc", "space")), P(("mc", "space"))),
        check_vma=False,
    )
```

```python
import functools
import math

import jax
import jax.numpy as jnp
from jax import lax
from jax.experimental import pallas as pl
from jax.experimental.pallas import tpu as pltpu
from jax.sharding import PartitionSpec as P

LANES = 128
MOST = 4
SUB = 16
NTAB = 64

TIME_STEP = 0.2
EARTH_SPIN = 0.0588
J2_COEF = 0.00108263
DRAG_SCALE = 0.008
SCALE_HEIGHT = 0.1
TABLE_TOP = 0.4
SPEED_FLOOR = 0.04
TINY = 1e-30
KEPT_VMEM = 8 << 20
KERNEL_VMEM = 32 << 20
LOG2_E = math.log2(math.e)

F32 = jnp.float32
BF = jnp.bfloat16


def unit_rows(blocks):
    return 5 * blocks + -(-blocks // (8 * LANES)) * 8


def lookup(table, index):
    dims = lax.GatherDimensionNumbers(
        offset_dims=(),
        collapsed_slice_dims=(1,),
        start_index_map=(1,),
        operand_batching_dims=(0,),
        start_indices_batching_dims=(0,),
    )
    mode = lax.GatherScatterMode.PROMISE_IN_BOUNDS
    return lax.gather(table, index[:, :, None], dims, (1, 1), mode=mode)


def substep(state, ballistic, table, slopes):
    x, y, z, dx, dy, dz = state
    zz = z * z
    radius_sq = x * x + y * y + zz
    inv = lax.rsqrt(radius_sq)
    radius = radius_sq * inv
    cells = (NTAB - 1) / TABLE_TOP
    coord = jnp.clip(radius * cells + (1.0 - cells), 0.0, NTAB + 1.0)
    index = coord.astype(jnp.int32)
    fraction = coord - index.astype(F32)
    fall = LOG2_E / SCALE_HEIGHT
    log_density = radius * -fall + (fall + math.log2(DRAG_SCALE))
    log_density = log_density + (lookup(table, index) + fraction * lookup(slopes, index))
    ux = dx + (TIME_STEP * EARTH_SPIN) * y
    uy = dy - (TIME_STEP * EARTH_SPIN) * x
    air_sq = ux * ux + uy * uy + dz * dz
    drag = jnp.exp2(log_density) * (ballistic * (air_sq * lax.rsqrt(jnp.maximum(air_sq, TINY))))
    inv_sq = inv * inv
    oblate = (1.5 * J2_COEF * TIME_STEP**2) * inv_sq
    base = TIME_STEP**2 - (5.0 * oblate) * (zz * inv_sq)
    inv_cube = inv_sq * inv
    pull = inv_cube * (base + oblate)
    pull_z = inv_cube * (base + 3.0 * oblate)
    dx = dx - x * pull - drag * ux
    dy = dy - y * pull - drag * uy
    dz = dz - z * pull_z - drag * dz
    return (x + dx, y + dy, z + dz, dx, dy, dz)


def propagate_kernel(table_hbm, orbit_hbm, props_hbm, cube_hbm, next_hbm, unit_ref, *scratch, group, unroll):
    table_ref, knots_ref, orbit_ref, props_ref, cube_ref, tiles, props, sem_in, sem_out = scratch
    blocks = orbit_ref.shape[1] // LANES
    rows = group * 8
    small = [
        pltpu.make_async_copy(table_hbm, table_ref, sem_in.at[0]),
        pltpu.make_async_copy(cube_hbm, cube_ref, sem_in.at[1]),
    ]
    knots_ref[...] = jnp.zeros((8, LANES), F32)
    for copy in small:
        copy.start()
    parts = range(blocks // rows)
    arrive, leave = [], []
    for i in parts:
        at = pl.ds(i * rows * LANES, rows * LANES)
        arrive.append(
            (
                pltpu.make_async_copy(orbit_hbm.at[:, at], orbit_ref.at[:, at], sem_in.at[2 + 2 * i]),
                pltpu.make_async_copy(props_hbm.at[:, at], props_ref.at[:, at], sem_in.at[3 + 2 * i]),
            )
        )
        leave.append(pltpu.make_async_copy(orbit_ref.at[:, at], next_hbm.at[:, at], sem_out.at[i]))
        for copy in arrive[i]:
            copy.start()
    for copy in small:
        copy.wait()
    knots_ref[pl.ds(0, 1), pl.ds(0, NTAB)] = table_ref[...] * LOG2_E
    knots = jnp.broadcast_to(knots_ref[pl.ds(0, 1), :], (8, LANES))
    table = pltpu.roll(knots, 1, 1)
    slopes = jnp.tile(knots - table, (group, 1))
    table = jnp.tile(table, (group, 1))
    unit_ref[pl.ds(5 * blocks, unit_ref.shape[0] - 5 * blocks), :] = jnp.zeros(
        (unit_ref.shape[0] - 5 * blocks, LANES), F32
    )
    unit_ref[pl.ds(5 * blocks, blocks // LANES), :] = cube_ref[...].astype(F32)
    for i in parts:
        for copy in arrive[i]:
            copy.wait()
        for b in range(rows):
            at = pl.ds((i * rows + b) * LANES, LANES)
            tiles[pl.ds(8 * b, 6), :] = orbit_ref[:, at]
            props[pl.ds(8 * b, 3), :] = props_ref[:, at]
        state = [tiles[pl.ds(c, rows, stride=8), :] for c in range(6)]
        state = (*state[:3], *(TIME_STEP * v for v in state[3:]))
        radius, weight, ballistic = (props[pl.ds(c, rows, stride=8), :] for c in range(3))
        unit_ref[pl.ds(3 * blocks + i * rows, rows), :] = radius
        unit_ref[pl.ds(4 * blocks + i * rows, rows), :] = weight
        state = lax.fori_loop(
            0, SUB, lambda k, s: substep(s, ballistic, table, slopes), state, unroll=unroll
        )
        state = (*state[:3], *((1.0 / TIME_STEP) * d for d in state[3:]))
        for c in range(6):
            tiles[pl.ds(c, rows, stride=8), :] = state[c]
        for c in range(3):
            unit_ref[pl.ds(c * blocks + i * rows, rows), :] = state[3 + c]
        for b in range(rows):
            orbit_ref[:, pl.ds((i * rows + b) * LANES, LANES)] = tiles[pl.ds(8 * b, 6), :]
        leave[i].start()
    for copy in leave:
        copy.wait()


def result(shape, dtype, resident):
    return pltpu.VMEM(shape, dtype) if resident else jax.ShapeDtypeStruct(shape, dtype)


def propagate(density_table, orbit_state, object_props, block_cube, resident):
    count = orbit_state.shape[1]
    blocks = count // LANES
    group = 16
    parts = blocks // (8 * group)
    cubes = block_cube.reshape(blocks // LANES, LANES)
    operands = (density_table.reshape(1, NTAB), orbit_state, object_props, cubes)
    return pl.pallas_call(
        functools.partial(propagate_kernel, group=group, unroll=4),
        in_specs=[pl.BlockSpec(memory_space=pltpu.HBM)] * 4,
        out_specs=(pl.BlockSpec(memory_space=pltpu.HBM), pl.BlockSpec(memory_space=pltpu.VMEM)),
        out_shape=(
            jax.ShapeDtypeStruct((6, count), F32),
            result((unit_rows(blocks), LANES), F32, resident),
        ),
        scratch_shapes=[
            pltpu.VMEM((1, NTAB), F32),
            pltpu.VMEM((8, LANES), F32),
            pltpu.VMEM((6, count), F32),
            pltpu.VMEM((3, count), F32),
            pltpu.VMEM((blocks // LANES, LANES), jnp.int32),
            pltpu.VMEM((64 * group, LANES), F32),
            pltpu.VMEM((64 * group, LANES), F32),
            pltpu.SemaphoreType.DMA((2 + 2 * parts,)),
            pltpu.SemaphoreType.DMA((parts,)),
        ],
        compiler_params=pltpu.CompilerParams(vmem_limit_bytes=KERNEL_VMEM) if resident else None,
        name="propagate",
    )(*(pltpu.with_memory_space_constraint(a, pltpu.HBM) for a in operands))


def split(a):
    high = a.astype(BF).astype(F32)
    return jnp.concatenate([high, a - high], 0).astype(BF)


def whole_tiles(rows):
    extra = -len(rows) % 8
    return jnp.concatenate([*rows, *([jnp.zeros((extra, LANES), F32)] if extra else [])], 0)


def partner_table(own_ids, mate_ids, most, own_first):
    none = float(len(mate_ids) * LANES)
    sub = lax.broadcasted_iota(jnp.int32, (LANES, LANES), 0).astype(F32)
    lane = lax.broadcasted_iota(jnp.int32, (LANES, LANES), 1).astype(F32)
    cols = whole_tiles(mate_ids).T
    found = []
    for h, own in enumerate(own_ids):
        places = [
            jnp.where(cols[:, t : t + 1] == own, sub + float(t * LANES), none) for t in range(len(mate_ids))
        ]
        if own_first:
            places[h] = jnp.where(sub == lane, none, places[h])
        last = jnp.full((1, LANES), -1.0, F32)
        hits = []
        for _ in range(most):
            best = None
            for place in places:
                later = jnp.where(place > last, place, none)
                best = later if best is None else jnp.minimum(best, later)
            last = jnp.min(best, axis=0, keepdims=True)
            hits.append(last)
        found.append(hits)
    counts = [sum((hit < none).astype(F32) for hit in hits) for hits in found]
    rows = counts + [hit for hits in found for hit in hits]
    turned = whole_tiles(rows).T
    halves = len(own_ids)
    ordered = [[0.0] * (most + 2) for _ in range(halves)]
    for h in range(halves):
        count = turned[:, h : h + 1]
        ahead = 0.0
        for g in range(halves):
            before = (lane + float(g * LANES)) < (sub + float(h * LANES))
            ahead = ahead + jnp.where((counts[g] > count) | ((counts[g] == count) & before), 1.0, 0.0)
        rank = jnp.sum(ahead, axis=1, keepdims=True)
        for q in range(halves):
            here = rank == lane + float(q * LANES)
            take = lambda v: jnp.sum(jnp.where(here, v, 0.0), axis=0, keepdims=True)
            ordered[q][0] += take(sub + float(h * LANES))
            ordered[q][1] += take(count)
            for p in range(most):
                at = halves + h * most + p
                ordered[q][2 + p] += take(turned[:, at : at + 1])
    rows = [ordered[q][k] for k in range(most + 2) for q in range(halves)]
    return whole_tiles(rows).astype(jnp.int32)


def pairs_kernel(*refs, arrays, first, last, own_too, most, group):
    own_ref, *mate_refs = refs[: 1 + arrays]
    refs = refs[1 + arrays :]
    if first:
        out_ref, lhs_ref, *refs = refs
    else:
        prev_ref, lhs_ref, out_ref, *refs = refs
    with_own = first or own_too
    own_tiles, mate_tiles, cols, table_vmem, table, table_sem = refs
    blocks = out_ref.shape[0]
    rows = unit_rows(blocks)
    halves = blocks // LANES
    units = [(ref, r) for ref in ((own_ref,) if with_own else ()) + tuple(mate_refs) for r in range(0, ref.shape[0], rows)]
    if not first:

        def ids(unit):
            ref, at = unit
            return [ref[pl.ds(at + 5 * blocks + h, 1), :] for h in range(halves)]

        table_vmem[...] = partner_table(ids((own_ref, 0)), [row for u in units for row in ids(u)], most, own_too)
        to_smem = pltpu.make_async_copy(table_vmem, table, table_sem.at[0])
        to_smem.start()
    cols[...] = jnp.zeros(cols.shape, F32)
    mate_tiles[pl.ds(len(units) * blocks * 8, 8), :] = jnp.zeros((8, LANES), F32)
    one = jnp.ones((8, LANES), F32)

    def planes(unit, i):
        ref, base = unit
        at = [pl.multiple_of(base + c * blocks + i * 8, 8) for c in range(5)]
        return [ref[pl.ds(a, 8), :] for a in at]

    def own_tile(i, carry):
        vx, vy, vz, rad, _ = planes((own_ref, 0), i)
        speed_sq = vx * vx + vy * vy + vz * vz
        for k, row in enumerate((-2.0 * vx, -2.0 * vy, -2.0 * vz, one, speed_sq, rad * rad, 2.0 * rad, one)):
            own_tiles[pl.ds(i * 64 + k, 8, stride=8), :] = row
        return carry

    if first:
        lax.fori_loop(0, blocks // 8, own_tile, 0, unroll=4)
    for n, unit in enumerate(units):

        def mate_tile(i, carry):
            vx, vy, vz, rad, wt = planes(unit, i)
            speed_sq = vx * vx + vy * vy + vz * vz + SPEED_FLOOR
            for k, row in enumerate((vx, vy, vz, speed_sq, one, wt, wt * rad, wt * rad * rad)):
                mate_tiles[pl.ds(n * blocks * 8 + i * 64 + k, 8, stride=8), :] = row
            return carry

        lax.fori_loop(0, blocks // 8, mate_tile, 0, unroll=4)
    if not first:
        to_smem.wait()
    lane = lax.broadcasted_iota(jnp.int32, (LANES, LANES), 1)
    is_gap = lax.broadcasted_iota(jnp.int32, (16, LANES), 0) % 8 < 5
    blank = jnp.zeros((16, LANES), BF)
    pad = jnp.zeros((96, LANES), BF)

    def run(q, place, count):
        for k in range(group):
            b = q * LANES + place + k if first else table[q, place + k]
            features = pl.ds(pl.multiple_of(b * LANES, LANES), LANES)
            if first:
                own = own_tiles[pl.ds(pl.multiple_of(b * 8, 8), 8), :]
                high = own.astype(BF).astype(F32)
                twice = [jnp.concatenate([part, part], 0).astype(BF) for part in (high, own - high)]
                lhs = jnp.concatenate([*twice, pad], 0).T
                lhs_ref[features, :] = lhs
            else:
                lhs = lhs_ref[features, :]
            acc = None
            for p in range(count):
                mate = b if first else table[(2 + p) * halves + q, place + k]
                parts = split(mate_tiles[pl.ds(pl.multiple_of(mate * 8, 8), 8), :])
                sides = []
                for side in (jnp.where(is_gap, parts, blank), jnp.where(is_gap, blank, parts)):
                    sides.append(jnp.concatenate([side, side, pad], 0))
                both = jnp.dot(lhs, jnp.concatenate(sides, 1), preferred_element_type=F32)
                gap = jnp.maximum(both[:, :LANES], SPEED_FLOOR)
                term = both[:, LANES:] * (gap * lax.rsqrt(gap))
                acc = term if acc is None else acc + term
            total = jnp.broadcast_to(jnp.sum(acc, axis=1, keepdims=True), (LANES, LANES))
            at = pl.multiple_of(jnp.bitwise_and(b, -LANES), LANES)
            pltpu.store(cols.at[pl.ds(at, LANES), :], total, mask=lane == jnp.bitwise_and(b, LANES - 1))

    def step(g, carry):
        q = g // (LANES // group)
        place = (g % (LANES // group)) * group
        if first:
            run(q, place, 1)
            return carry
        longest = table[halves + q, place]
        for count in range(1, most + 1):

            @pl.when(longest == count)
            def _():
                run(q, place, count)

        return carry

    lax.fori_loop(0, blocks // group, step, 0)
    for h in range(halves):
        at = pl.ds(h * LANES, LANES)
        total = cols[at, :].T
        rad = own_ref[pl.ds(3 * blocks + h * LANES, LANES), :]
        wt = own_ref[pl.ds(4 * blocks + h * LANES, LANES), :]
        if first:
            total = total - (4.0 * SPEED_FLOOR**0.5) * wt * rad * rad
        else:
            total = total + prev_ref[at, :]
        if last:
            total = wt * total * (1.0 / (MOST * LANES))
        out_ref[at, :] = total


def pairs(own, mates, prev, lhs, own_too, last, resident):
    rows = own.shape[0]
    blocks = rows // 5 // LANES * LANES
    first = prev is None
    most = MOST - 1
    units = sum(a.shape[0] for a in mates) // rows + (1 if first or own_too else 0)
    table = -(-(most + 2) * (blocks // LANES) // 8) * 8
    operands = [own, *mates, *(() if first else (prev, lhs))]
    total = result((blocks, LANES), F32, resident and not last)
    if resident:
        operands = [pltpu.with_memory_space_constraint(a, pltpu.VMEM) for a in operands]
    return pl.pallas_call(
        functools.partial(
            pairs_kernel,
            arrays=len(mates),
            first=first,
            last=last,
            own_too=own_too,
            most=most,
            group=64 if first else 32,
        ),
        in_specs=[pl.BlockSpec(memory_space=pltpu.VMEM)] * len(operands),
        out_shape=(total, result((blocks * LANES, LANES), BF, resident)) if first else total,
        scratch_shapes=[
            pltpu.VMEM((blocks * 8, LANES), F32),
            pltpu.VMEM(((units * blocks + 1) * 8, LANES), F32),
            pltpu.VMEM((blocks, LANES), F32),
            pltpu.VMEM((table, LANES), jnp.int32),
            pltpu.SMEM((table, LANES), jnp.int32),
            pltpu.SemaphoreType.DMA((1,)),
        ],
        compiler_params=pltpu.CompilerParams(vmem_limit_bytes=KERNEL_VMEM) if resident else None,
        name="pairs",
    )(*operands)


def exchange(own, size):
    def send(a, bit_of):
        return lax.ppermute(a, "space", [(i, i ^ bit_of(i)) for i in range(size)])

    def beside(i):
        return 1

    mate = send(own, beside)
    bits = [1 << k for k in range(1, size.bit_length() - 1)]
    if len(bits) == 2:
        def across(i):
            return bits[i % 2]

        far = send(own, across)
        far_mate = send(mate, across)
        far_beside = send(far, beside)
        corner = send(far_beside, across)
        far_mate_beside = send(far_mate, beside)
        corner_beside = send(corner, beside)
        return [[mate, far, far_beside], [far_mate, far_mate_beside, corner, corner_beside]]
    held = [own, mate]
    for bit in bits:
        held.append(send(jnp.concatenate(held, 0), lambda i: bit))
    return [[mate], held[2:]]


def on_device(orbit_state, object_props, density_table, block_cube):
    size = lax.axis_size("space")
    blocks = block_cube.shape[0]
    resident = size * unit_rows(blocks) * LANES * 4 <= KEPT_VMEM
    next_state, own = propagate(density_table, orbit_state, object_props, block_cube, resident)
    groups = exchange(own, size)
    total, lhs = pairs(own, [], None, None, False, False, resident)
    for k, mates in enumerate(groups):
        total = pairs(own, mates, total, lhs, k == 0, k == len(groups) - 1, resident)
    return (next_state, total.reshape(orbit_state.shape[1]))


def solution(mesh):
    placed = (P(None, ("mc", "space")), P(None, ("mc", "space")), P(), P(("mc", "space")))
    return jax.shard_map(
        on_device,
        mesh=mesh,
        in_specs=placed,
        out_specs=(P(None, ("mc", "space")), P(("mc", "space"))),
        check_vma=False,
    )
```

```python
import functools
import math

import jax
import jax.numpy as jnp
from jax import lax
from jax.experimental import pallas as pl
from jax.experimental.pallas import tpu as pltpu
from jax.sharding import PartitionSpec as P

LANES = 128
MOST = 4
SUB = 16
NTAB = 64

TIME_STEP = 0.2
EARTH_SPIN = 0.0588
J2_COEF = 0.00108263
DRAG_SCALE = 0.008
SCALE_HEIGHT = 0.1
TABLE_TOP = 0.4
SPEED_FLOOR = 0.04
TINY = 1e-30
KEPT_VMEM = 8 << 20
KERNEL_VMEM = 32 << 20
LOG2_E = math.log2(math.e)

F32 = jnp.float32
BF = jnp.bfloat16


def unit_rows(blocks):
    return 5 * blocks + -(-blocks // (8 * LANES)) * 8


def lookup(table, index):
    dims = lax.GatherDimensionNumbers(
        offset_dims=(),
        collapsed_slice_dims=(1,),
        start_index_map=(1,),
        operand_batching_dims=(0,),
        start_indices_batching_dims=(0,),
    )
    mode = lax.GatherScatterMode.PROMISE_IN_BOUNDS
    return lax.gather(table, index[:, :, None], dims, (1, 1), mode=mode)


def substep(state, ballistic, table, slopes):
    x, y, z, dx, dy, dz = state
    zz = z * z
    radius_sq = x * x + y * y + zz
    inv = lax.rsqrt(radius_sq)
    radius = radius_sq * inv
    cells = (NTAB - 1) / TABLE_TOP
    coord = jnp.clip(radius * cells + (1.0 - cells), 0.0, NTAB + 1.0)
    index = coord.astype(jnp.int32)
    fraction = coord - index.astype(F32)
    fall = LOG2_E / SCALE_HEIGHT
    log_density = radius * -fall + (fall + math.log2(DRAG_SCALE))
    log_density = log_density + (lookup(table, index) + fraction * lookup(slopes, index))
    ux = dx + (TIME_STEP * EARTH_SPIN) * y
    uy = dy - (TIME_STEP * EARTH_SPIN) * x
    air_sq = ux * ux + uy * uy + dz * dz
    drag = jnp.exp2(log_density) * (ballistic * (air_sq * lax.rsqrt(jnp.maximum(air_sq, TINY))))
    inv_sq = inv * inv
    oblate = (1.5 * J2_COEF * TIME_STEP**2) * inv_sq
    base = TIME_STEP**2 - (5.0 * oblate) * (zz * inv_sq)
    inv_cube = inv_sq * inv
    pull = inv_cube * (base + oblate)
    pull_z = inv_cube * (base + 3.0 * oblate)
    dx = dx - x * pull - drag * ux
    dy = dy - y * pull - drag * uy
    dz = dz - z * pull_z - drag * dz
    return (x + dx, y + dy, z + dz, dx, dy, dz)


def propagate_kernel(table_hbm, orbit_hbm, props_hbm, cube_hbm, next_ref, unit_ref, *scratch, group, unroll):
    table_ref, knots_ref, orbit_ref, props_ref, cube_ref, tiles, props, sem_in = scratch
    blocks = orbit_ref.shape[1] // LANES
    rows = group * 8
    small = [
        pltpu.make_async_copy(table_hbm, table_ref, sem_in.at[0]),
        pltpu.make_async_copy(cube_hbm, cube_ref, sem_in.at[1]),
    ]
    knots_ref[...] = jnp.zeros((8, LANES), F32)
    for copy in small:
        copy.start()
    parts = range(blocks // rows)
    arrive = []
    for i in parts:
        at = pl.ds(i * rows * LANES, rows * LANES)
        arrive.append(
            (
                pltpu.make_async_copy(orbit_hbm.at[:, at], orbit_ref.at[:, at], sem_in.at[2 + 2 * i]),
                pltpu.make_async_copy(props_hbm.at[:, at], props_ref.at[:, at], sem_in.at[3 + 2 * i]),
            )
        )
        for copy in arrive[i]:
            copy.start()
    for copy in small:
        copy.wait()
    knots_ref[pl.ds(0, 1), pl.ds(0, NTAB)] = table_ref[...] * LOG2_E
    knots = jnp.broadcast_to(knots_ref[pl.ds(0, 1), :], (8, LANES))
    table = pltpu.roll(knots, 1, 1)
    slopes = jnp.tile(knots - table, (group, 1))
    table = jnp.tile(table, (group, 1))
    unit_ref[pl.ds(5 * blocks, unit_ref.shape[0] - 5 * blocks), :] = jnp.zeros(
        (unit_ref.shape[0] - 5 * blocks, LANES), F32
    )
    unit_ref[pl.ds(5 * blocks, blocks // LANES), :] = cube_ref[...].astype(F32)
    for i in parts:
        for copy in arrive[i]:
            copy.wait()
        for b in range(rows):
            at = pl.ds((i * rows + b) * LANES, LANES)
            tiles[pl.ds(8 * b, 6), :] = orbit_ref[:, at]
            props[pl.ds(8 * b, 3), :] = props_ref[:, at]
        state = [tiles[pl.ds(c, rows, stride=8), :] for c in range(6)]
        state = (*state[:3], *(TIME_STEP * v for v in state[3:]))
        radius, weight, ballistic = (props[pl.ds(c, rows, stride=8), :] for c in range(3))
        unit_ref[pl.ds(3 * blocks + i * rows, rows), :] = radius
        unit_ref[pl.ds(4 * blocks + i * rows, rows), :] = weight
        state = lax.fori_loop(
            0, SUB, lambda k, s: substep(s, ballistic, table, slopes), state, unroll=unroll
        )
        state = (*state[:3], *((1.0 / TIME_STEP) * d for d in state[3:]))
        for c in range(6):
            tiles[pl.ds(c, rows, stride=8), :] = state[c]
        for c in range(3):
            unit_ref[pl.ds(c * blocks + i * rows, rows), :] = state[3 + c]
        for b in range(rows):
            next_ref[:, pl.ds((i * rows + b) * LANES, LANES)] = tiles[pl.ds(8 * b, 6), :]


def result(shape, dtype, resident):
    return pltpu.VMEM(shape, dtype) if resident else jax.ShapeDtypeStruct(shape, dtype)


def propagate(density_table, orbit_state, object_props, block_cube, resident):
    count = orbit_state.shape[1]
    blocks = count // LANES
    group = 16
    parts = blocks // (8 * group)
    cubes = block_cube.reshape(blocks // LANES, LANES)
    operands = (density_table.reshape(1, NTAB), orbit_state, object_props, cubes)
    return pl.pallas_call(
        functools.partial(propagate_kernel, group=group, unroll=4),
        in_specs=[pl.BlockSpec(memory_space=pltpu.HBM)] * 4,
        out_specs=(pl.BlockSpec(memory_space=pltpu.VMEM),) * 2,
        out_shape=(
            result((6, count), F32, resident),
            result((unit_rows(blocks), LANES), F32, resident),
        ),
        scratch_shapes=[
            pltpu.VMEM((1, NTAB), F32),
            pltpu.VMEM((8, LANES), F32),
            pltpu.VMEM((6, count), F32),
            pltpu.VMEM((3, count), F32),
            pltpu.VMEM((blocks // LANES, LANES), jnp.int32),
            pltpu.VMEM((64 * group, LANES), F32),
            pltpu.VMEM((64 * group, LANES), F32),
            pltpu.SemaphoreType.DMA((2 + 2 * parts,)),
        ],
        compiler_params=pltpu.CompilerParams(vmem_limit_bytes=KERNEL_VMEM) if resident else None,
        name="propagate",
    )(*(pltpu.with_memory_space_constraint(a, pltpu.HBM) for a in operands))


def split(a):
    high = a.astype(BF).astype(F32)
    return jnp.concatenate([high, a - high], 0).astype(BF)


def whole_tiles(rows):
    extra = -len(rows) % 8
    return jnp.concatenate([*rows, *([jnp.zeros((extra, LANES), F32)] if extra else [])], 0)


def partner_table(own_ids, mate_ids, most, own_first):
    none = float(len(mate_ids) * LANES)
    sub = lax.broadcasted_iota(jnp.int32, (LANES, LANES), 0).astype(F32)
    lane = lax.broadcasted_iota(jnp.int32, (LANES, LANES), 1).astype(F32)
    cols = whole_tiles(mate_ids).T
    found = []
    for h, own in enumerate(own_ids):
        places = [
            jnp.where(cols[:, t : t + 1] == own, sub + float(t * LANES), none) for t in range(len(mate_ids))
        ]
        if own_first:
            places[h] = jnp.where(sub == lane, none, places[h])
        last = jnp.full((1, LANES), -1.0, F32)
        hits = []
        for _ in range(most):
            best = None
            for place in places:
                later = jnp.where(place > last, place, none)
                best = later if best is None else jnp.minimum(best, later)
            last = jnp.min(best, axis=0, keepdims=True)
            hits.append(last)
        found.append(hits)
    counts = [sum((hit < none).astype(F32) for hit in hits) for hits in found]
    rows = counts + [hit for hits in found for hit in hits]
    turned = whole_tiles(rows).T
    halves = len(own_ids)
    ordered = [[0.0] * (most + 2) for _ in range(halves)]
    for h in range(halves):
        count = turned[:, h : h + 1]
        ahead = 0.0
        for g in range(halves):
            before = (lane + float(g * LANES)) < (sub + float(h * LANES))
            ahead = ahead + jnp.where((counts[g] > count) | ((counts[g] == count) & before), 1.0, 0.0)
        rank = jnp.sum(ahead, axis=1, keepdims=True)
        for q in range(halves):
            here = rank == lane + float(q * LANES)
            take = lambda v: jnp.sum(jnp.where(here, v, 0.0), axis=0, keepdims=True)
            ordered[q][0] += take(sub + float(h * LANES))
            ordered[q][1] += take(count)
            for p in range(most):
                at = halves + h * most + p
                ordered[q][2 + p] += take(turned[:, at : at + 1])
    rows = [ordered[q][k] for k in range(most + 2) for q in range(halves)]
    return whole_tiles(rows).astype(jnp.int32)


def pairs_kernel(*refs, arrays, first, last, own_too, most, group):
    own_ref, *mate_refs = refs[: 1 + arrays]
    refs = refs[1 + arrays :]
    if first:
        moved_ref, out_ref, lhs_ref, next_hbm, *refs = refs
    else:
        prev_ref, lhs_ref, out_ref, *refs = refs
    with_own = first or own_too
    own_tiles, mate_tiles, cols, table_vmem, table, table_sem = refs
    if first:
        store_next = pltpu.make_async_copy(moved_ref, next_hbm, table_sem.at[0])
        store_next.start()
    blocks = out_ref.shape[0]
    rows = unit_rows(blocks)
    halves = blocks // LANES
    units = [(ref, r) for ref in ((own_ref,) if with_own else ()) + tuple(mate_refs) for r in range(0, ref.shape[0], rows)]
    if not first:

        def ids(unit):
            ref, at = unit
            return [ref[pl.ds(at + 5 * blocks + h, 1), :] for h in range(halves)]

        table_vmem[...] = partner_table(ids((own_ref, 0)), [row for u in units for row in ids(u)], most, own_too)
        to_smem = pltpu.make_async_copy(table_vmem, table, table_sem.at[0])
        to_smem.start()
    cols[...] = jnp.zeros(cols.shape, F32)
    mate_tiles[pl.ds(len(units) * blocks * 8, 8), :] = jnp.zeros((8, LANES), F32)
    one = jnp.ones((8, LANES), F32)

    def planes(unit, i):
        ref, base = unit
        at = [pl.multiple_of(base + c * blocks + i * 8, 8) for c in range(5)]
        return [ref[pl.ds(a, 8), :] for a in at]

    def own_tile(i, carry):
        vx, vy, vz, rad, _ = planes((own_ref, 0), i)
        speed_sq = vx * vx + vy * vy + vz * vz
        for k, row in enumerate((-2.0 * vx, -2.0 * vy, -2.0 * vz, one, speed_sq, rad * rad, 2.0 * rad, one)):
            own_tiles[pl.ds(i * 64 + k, 8, stride=8), :] = row
        return carry

    if first:
        lax.fori_loop(0, blocks // 8, own_tile, 0, unroll=4)
    for n, unit in enumerate(units):

        def mate_tile(i, carry):
            vx, vy, vz, rad, wt = planes(unit, i)
            speed_sq = vx * vx + vy * vy + vz * vz + SPEED_FLOOR
            for k, row in enumerate((vx, vy, vz, speed_sq, one, wt, wt * rad, wt * rad * rad)):
                mate_tiles[pl.ds(n * blocks * 8 + i * 64 + k, 8, stride=8), :] = row
            return carry

        lax.fori_loop(0, blocks // 8, mate_tile, 0, unroll=4)
    if not first:
        to_smem.wait()
    lane = lax.broadcasted_iota(jnp.int32, (LANES, LANES), 1)
    is_gap = lax.broadcasted_iota(jnp.int32, (16, LANES), 0) % 8 < 5
    blank = jnp.zeros((16, LANES), BF)
    pad = jnp.zeros((96, LANES), BF)

    def run(q, place, count):
        for k in range(group):
            b = q * LANES + place + k if first else table[q, place + k]
            features = pl.ds(pl.multiple_of(b * LANES, LANES), LANES)
            if first:
                own = own_tiles[pl.ds(pl.multiple_of(b * 8, 8), 8), :]
                high = own.astype(BF).astype(F32)
                twice = [jnp.concatenate([part, part], 0).astype(BF) for part in (high, own - high)]
                lhs = jnp.concatenate([*twice, pad], 0).T
                lhs_ref[features, :] = lhs
            else:
                lhs = lhs_ref[features, :]
            acc = None
            for p in range(count):
                mate = b if first else table[(2 + p) * halves + q, place + k]
                parts = split(mate_tiles[pl.ds(pl.multiple_of(mate * 8, 8), 8), :])
                sides = []
                for side in (jnp.where(is_gap, parts, blank), jnp.where(is_gap, blank, parts)):
                    sides.append(jnp.concatenate([side, side, pad], 0))
                both = jnp.dot(lhs, jnp.concatenate(sides, 1), preferred_element_type=F32)
                gap = jnp.maximum(both[:, :LANES], SPEED_FLOOR)
                term = both[:, LANES:] * (gap * lax.rsqrt(gap))
                acc = term if acc is None else acc + term
            total = jnp.broadcast_to(jnp.sum(acc, axis=1, keepdims=True), (LANES, LANES))
            at = pl.multiple_of(jnp.bitwise_and(b, -LANES), LANES)
            pltpu.store(cols.at[pl.ds(at, LANES), :], total, mask=lane == jnp.bitwise_and(b, LANES - 1))

    def step(g, carry):
        q = g // (LANES // group)
        place = (g % (LANES // group)) * group
        if first:
            run(q, place, 1)
            return carry
        longest = table[halves + q, place]
        for count in range(1, most + 1):

            @pl.when(longest == count)
            def _():
                run(q, place, count)

        return carry

    lax.fori_loop(0, blocks // group, step, 0)
    for h in range(halves):
        at = pl.ds(h * LANES, LANES)
        total = cols[at, :].T
        rad = own_ref[pl.ds(3 * blocks + h * LANES, LANES), :]
        wt = own_ref[pl.ds(4 * blocks + h * LANES, LANES), :]
        if first:
            total = total - (4.0 * SPEED_FLOOR**0.5) * wt * rad * rad
        else:
            total = total + prev_ref[at, :]
        if last:
            total = wt * total * (1.0 / (MOST * LANES))
        out_ref[at, :] = total
    if first:
        store_next.wait()


def pairs(own, mates, prev, lhs, own_too, last, resident, moved=None):
    rows = own.shape[0]
    blocks = rows // 5 // LANES * LANES
    first = prev is None
    most = MOST - 1
    units = sum(a.shape[0] for a in mates) // rows + (1 if first or own_too else 0)
    table = -(-(most + 2) * (blocks // LANES) // 8) * 8
    operands = [own, *mates, *((moved,) if first else (prev, lhs))]
    total = result((blocks, LANES), F32, resident and not last)
    vmem = pl.BlockSpec(memory_space=pltpu.VMEM)
    if first:
        features = result((blocks * LANES, LANES), BF, resident)
        out_shape = (total, features, jax.ShapeDtypeStruct(moved.shape, F32))
        out_specs = (vmem, vmem, pl.BlockSpec(memory_space=pltpu.HBM))
    else:
        out_shape, out_specs = total, vmem
    if resident:
        operands = [pltpu.with_memory_space_constraint(a, pltpu.VMEM) for a in operands]
    return pl.pallas_call(
        functools.partial(
            pairs_kernel,
            arrays=len(mates),
            first=first,
            last=last,
            own_too=own_too,
            most=most,
            group=64 if first else 32,
        ),
        in_specs=[vmem] * len(operands),
        out_specs=out_specs,
        out_shape=out_shape,
        scratch_shapes=[
            pltpu.VMEM((blocks * 8, LANES), F32),
            pltpu.VMEM(((units * blocks + 1) * 8, LANES), F32),
            pltpu.VMEM((blocks, LANES), F32),
            pltpu.VMEM((table, LANES), jnp.int32),
            pltpu.SMEM((table, LANES), jnp.int32),
            pltpu.SemaphoreType.DMA((1,)),
        ],
        compiler_params=pltpu.CompilerParams(vmem_limit_bytes=KERNEL_VMEM) if resident else None,
        name="pairs",
    )(*operands)


def exchange(own, size):
    def send(a, bit_of):
        return lax.ppermute(a, "space", [(i, i ^ bit_of(i)) for i in range(size)])

    def beside(i):
        return 1

    mate = send(own, beside)
    bits = [1 << k for k in range(1, size.bit_length() - 1)]
    if len(bits) == 2:
        def across(i):
            return bits[i % 2]

        far = send(own, across)
        far_mate = send(mate, across)
        far_beside = send(far, beside)
        corner = send(far_beside, across)
        far_mate_beside = send(far_mate, beside)
        corner_beside = send(corner, beside)
        return [[mate, far, far_beside, far_mate], [far_mate_beside, corner, corner_beside]]
    held = [own, mate]
    for bit in bits:
        held.append(send(jnp.concatenate(held, 0), lambda i: bit))
    return [[mate], held[2:]]


def on_device(orbit_state, object_props, density_table, block_cube):
    size = lax.axis_size("space")
    blocks = block_cube.shape[0]
    resident = size * unit_rows(blocks) * LANES * 4 <= KEPT_VMEM
    moved, own = propagate(density_table, orbit_state, object_props, block_cube, resident)
    groups = exchange(own, size)
    total, lhs, next_state = pairs(own, [], None, None, False, False, resident, moved)
    for k, mates in enumerate(groups):
        total = pairs(own, mates, total, lhs, k == 0, k == len(groups) - 1, resident)
    return (next_state, total.reshape(orbit_state.shape[1]))


def solution(mesh):
    placed = (P(None, ("mc", "space")), P(None, ("mc", "space")), P(), P(("mc", "space")))
    return jax.shard_map(
        on_device,
        mesh=mesh,
        in_specs=placed,
        out_specs=(P(None, ("mc", "space")), P(("mc", "space"))),
        check_vma=False,
    )
```

```python
import functools
import math

import jax
import jax.numpy as jnp
from jax import lax
from jax.experimental import pallas as pl
from jax.experimental.pallas import tpu as pltpu
from jax.sharding import PartitionSpec as P

LANES = 128
MOST = 4
SUB = 16
NTAB = 64

TIME_STEP = 0.2
EARTH_SPIN = 0.0588
J2_COEF = 0.00108263
DRAG_SCALE = 0.008
SCALE_HEIGHT = 0.1
TABLE_TOP = 0.4
SPEED_FLOOR = 0.04
TINY = 1e-30
KEPT_VMEM = 8 << 20
KERNEL_VMEM = 32 << 20
LOG2_E = math.log2(math.e)

F32 = jnp.float32
BF = jnp.bfloat16


def unit_rows(blocks):
    return 5 * blocks + -(-blocks // (8 * LANES)) * 8


def lookup(table, index):
    dims = lax.GatherDimensionNumbers(
        offset_dims=(),
        collapsed_slice_dims=(1,),
        start_index_map=(1,),
        operand_batching_dims=(0,),
        start_indices_batching_dims=(0,),
    )
    mode = lax.GatherScatterMode.PROMISE_IN_BOUNDS
    return lax.gather(table, index[:, :, None], dims, (1, 1), mode=mode)


def substep(state, ballistic, table, slopes):
    x, y, z, dx, dy, dz = state
    zz = z * z
    radius_sq = x * x + y * y + zz
    inv = lax.rsqrt(radius_sq)
    radius = radius_sq * inv
    cells = (NTAB - 1) / TABLE_TOP
    coord = jnp.clip(radius * cells + (1.0 - cells), 0.0, NTAB + 1.0)
    index = coord.astype(jnp.int32)
    fraction = coord - index.astype(F32)
    fall = LOG2_E / SCALE_HEIGHT
    log_density = radius * -fall + (fall + math.log2(DRAG_SCALE))
    log_density = log_density + (lookup(table, index) + fraction * lookup(slopes, index))
    ux = dx + (TIME_STEP * EARTH_SPIN) * y
    uy = dy - (TIME_STEP * EARTH_SPIN) * x
    air_sq = ux * ux + uy * uy + dz * dz
    drag = jnp.exp2(log_density) * (ballistic * (air_sq * lax.rsqrt(jnp.maximum(air_sq, TINY))))
    inv_sq = inv * inv
    oblate = (1.5 * J2_COEF * TIME_STEP**2) * inv_sq
    base = TIME_STEP**2 - (5.0 * oblate) * (zz * inv_sq)
    inv_cube = inv_sq * inv
    pull = inv_cube * (base + oblate)
    pull_z = inv_cube * (base + 3.0 * oblate)
    dx = dx - x * pull - drag * ux
    dy = dy - y * pull - drag * uy
    dz = dz - z * pull_z - drag * dz
    return (x + dx, y + dy, z + dz, dx, dy, dz)


def propagate_kernel(table_hbm, orbit_hbm, props_hbm, cube_hbm, next_ref, unit_ref, *scratch, group, unroll):
    table_ref, knots_ref, orbit_ref, props_ref, cube_ref, tiles, props, sem_in = scratch
    blocks = orbit_ref.shape[1] // LANES
    rows = group * 8
    small = [
        pltpu.make_async_copy(table_hbm, table_ref, sem_in.at[0]),
        pltpu.make_async_copy(cube_hbm, cube_ref, sem_in.at[1]),
    ]
    knots_ref[...] = jnp.zeros((8, LANES), F32)
    for copy in small:
        copy.start()
    parts = range(blocks // rows)
    arrive = []
    for i in parts:
        at = pl.ds(i * rows * LANES, rows * LANES)
        arrive.append(
            (
                pltpu.make_async_copy(orbit_hbm.at[:, at], orbit_ref.at[:, at], sem_in.at[2 + 2 * i]),
                pltpu.make_async_copy(props_hbm.at[:, at], props_ref.at[:, at], sem_in.at[3 + 2 * i]),
            )
        )
        for copy in arrive[i]:
            copy.start()
    for copy in small:
        copy.wait()
    knots_ref[pl.ds(0, 1), pl.ds(0, NTAB)] = table_ref[...] * LOG2_E
    knots = jnp.broadcast_to(knots_ref[pl.ds(0, 1), :], (8, LANES))
    table = pltpu.roll(knots, 1, 1)
    slopes = jnp.tile(knots - table, (group, 1))
    table = jnp.tile(table, (group, 1))
    unit_ref[pl.ds(5 * blocks, unit_ref.shape[0] - 5 * blocks), :] = jnp.zeros(
        (unit_ref.shape[0] - 5 * blocks, LANES), F32
    )
    unit_ref[pl.ds(5 * blocks, blocks // LANES), :] = cube_ref[...].astype(F32)
    for i in parts:
        for copy in arrive[i]:
            copy.wait()
        for b in range(rows):
            at = pl.ds((i * rows + b) * LANES, LANES)
            tiles[pl.ds(8 * b, 6), :] = orbit_ref[:, at]
            props[pl.ds(8 * b, 3), :] = props_ref[:, at]
        state = [tiles[pl.ds(c, rows, stride=8), :] for c in range(6)]
        state = (*state[:3], *(TIME_STEP * v for v in state[3:]))
        radius, weight, ballistic = (props[pl.ds(c, rows, stride=8), :] for c in range(3))
        unit_ref[pl.ds(3 * blocks + i * rows, rows), :] = radius
        unit_ref[pl.ds(4 * blocks + i * rows, rows), :] = weight
        state = lax.fori_loop(
            0, SUB, lambda k, s: substep(s, ballistic, table, slopes), state, unroll=unroll
        )
        state = (*state[:3], *((1.0 / TIME_STEP) * d for d in state[3:]))
        for c in range(6):
            tiles[pl.ds(c, rows, stride=8), :] = state[c]
        for c in range(3):
            unit_ref[pl.ds(c * blocks + i * rows, rows), :] = state[3 + c]
        for b in range(rows):
            next_ref[:, pl.ds((i * rows + b) * LANES, LANES)] = tiles[pl.ds(8 * b, 6), :]


def result(shape, dtype, resident):
    return pltpu.VMEM(shape, dtype) if resident else jax.ShapeDtypeStruct(shape, dtype)


def propagate(density_table, orbit_state, object_props, block_cube, resident):
    count = orbit_state.shape[1]
    blocks = count // LANES
    group = 16
    parts = blocks // (8 * group)
    cubes = block_cube.reshape(blocks // LANES, LANES)
    operands = (density_table.reshape(1, NTAB), orbit_state, object_props, cubes)
    return pl.pallas_call(
        functools.partial(propagate_kernel, group=group, unroll=4),
        in_specs=[pl.BlockSpec(memory_space=pltpu.HBM)] * 4,
        out_specs=(pl.BlockSpec(memory_space=pltpu.VMEM),) * 2,
        out_shape=(
            result((6, count), F32, resident),
            result((unit_rows(blocks), LANES), F32, resident),
        ),
        scratch_shapes=[
            pltpu.VMEM((1, NTAB), F32),
            pltpu.VMEM((8, LANES), F32),
            pltpu.VMEM((6, count), F32),
            pltpu.VMEM((3, count), F32),
            pltpu.VMEM((blocks // LANES, LANES), jnp.int32),
            pltpu.VMEM((64 * group, LANES), F32),
            pltpu.VMEM((64 * group, LANES), F32),
            pltpu.SemaphoreType.DMA((2 + 2 * parts,)),
        ],
        compiler_params=pltpu.CompilerParams(vmem_limit_bytes=KERNEL_VMEM) if resident else None,
        name="propagate",
    )(*(pltpu.with_memory_space_constraint(a, pltpu.HBM) for a in operands))


def split(a):
    high = a.astype(BF).astype(F32)
    return jnp.concatenate([high, a - high], 0).astype(BF)


def whole_tiles(rows):
    extra = -len(rows) % 8
    return jnp.concatenate([*rows, *([jnp.zeros((extra, LANES), F32)] if extra else [])], 0)


def partner_table(own_ids, mate_ids, most, own_first):
    none = float(len(mate_ids) * LANES)
    sub = lax.broadcasted_iota(jnp.int32, (LANES, LANES), 0).astype(F32)
    lane = lax.broadcasted_iota(jnp.int32, (LANES, LANES), 1).astype(F32)
    cols = whole_tiles(mate_ids).T
    found = []
    for h, own in enumerate(own_ids):
        places = [
            jnp.where(cols[:, t : t + 1] == own, sub + float(t * LANES), none) for t in range(len(mate_ids))
        ]
        if own_first:
            places[h] = jnp.where(sub == lane, none, places[h])
        last = jnp.full((1, LANES), -1.0, F32)
        hits = []
        for _ in range(most):
            best = None
            for place in places:
                later = jnp.where(place > last, place, none)
                best = later if best is None else jnp.minimum(best, later)
            last = jnp.min(best, axis=0, keepdims=True)
            hits.append(last)
        found.append(hits)
    counts = [sum((hit < none).astype(F32) for hit in hits) for hits in found]
    rows = counts + [hit for hits in found for hit in hits]
    turned = whole_tiles(rows).T
    halves = len(own_ids)
    ordered = [[0.0] * (most + 2) for _ in range(halves)]
    for h in range(halves):
        count = turned[:, h : h + 1]
        ahead = 0.0
        for g in range(halves):
            before = (lane + float(g * LANES)) < (sub + float(h * LANES))
            ahead = ahead + jnp.where((counts[g] > count) | ((counts[g] == count) & before), 1.0, 0.0)
        rank = jnp.sum(ahead, axis=1, keepdims=True)
        for q in range(halves):
            here = rank == lane + float(q * LANES)
            take = lambda v: jnp.sum(jnp.where(here, v, 0.0), axis=0, keepdims=True)
            ordered[q][0] += take(sub + float(h * LANES))
            ordered[q][1] += take(count)
            for p in range(most):
                at = halves + h * most + p
                ordered[q][2 + p] += take(turned[:, at : at + 1])
    rows = [ordered[q][k] for k in range(most + 2) for q in range(halves)]
    return whole_tiles(rows).astype(jnp.int32)


def pairs_kernel(*refs, arrays, first, last, own_too, most, group):
    own_ref, *mate_refs = refs[: 1 + arrays]
    refs = refs[1 + arrays :]
    if first:
        moved_ref, out_ref, lhs_ref, next_hbm, *refs = refs
    else:
        prev_ref, lhs_ref, out_ref, *refs = refs
    with_own = first or own_too
    own_tiles, mate_tiles, cols, table_vmem, table, table_sem = refs
    if first:
        store_next = pltpu.make_async_copy(moved_ref, next_hbm, table_sem.at[0])
        store_next.start()
    blocks = out_ref.shape[0]
    rows = unit_rows(blocks)
    halves = blocks // LANES
    units = [(ref, r) for ref in ((own_ref,) if with_own else ()) + tuple(mate_refs) for r in range(0, ref.shape[0], rows)]
    if not first:

        def ids(unit):
            ref, at = unit
            return [ref[pl.ds(at + 5 * blocks + h, 1), :] for h in range(halves)]

        table_vmem[...] = partner_table(ids((own_ref, 0)), [row for u in units for row in ids(u)], most, own_too)
        to_smem = pltpu.make_async_copy(table_vmem, table, table_sem.at[0])
        to_smem.start()
    cols[...] = jnp.zeros(cols.shape, F32)
    mate_tiles[pl.ds(len(units) * blocks * 8, 8), :] = jnp.zeros((8, LANES), F32)
    one = jnp.ones((8, LANES), F32)

    def planes(unit, i):
        ref, base = unit
        at = [pl.multiple_of(base + c * blocks + i * 8, 8) for c in range(5)]
        return [ref[pl.ds(a, 8), :] for a in at]

    def own_tile(i, carry):
        vx, vy, vz, rad, _ = planes((own_ref, 0), i)
        speed_sq = vx * vx + vy * vy + vz * vz
        for k, row in enumerate((-2.0 * vx, -2.0 * vy, -2.0 * vz, one, speed_sq, rad * rad, 2.0 * rad, one)):
            own_tiles[pl.ds(i * 64 + k, 8, stride=8), :] = row
        return carry

    if first:
        lax.fori_loop(0, blocks // 8, own_tile, 0, unroll=4)
    for n, unit in enumerate(units):

        def mate_tile(i, carry):
            vx, vy, vz, rad, wt = planes(unit, i)
            speed_sq = vx * vx + vy * vy + vz * vz + SPEED_FLOOR
            for k, row in enumerate((vx, vy, vz, speed_sq, one, wt, wt * rad, wt * rad * rad)):
                mate_tiles[pl.ds(n * blocks * 8 + i * 64 + k, 8, stride=8), :] = row
            return carry

        lax.fori_loop(0, blocks // 8, mate_tile, 0, unroll=4)
    if not first:
        to_smem.wait()
    lane = lax.broadcasted_iota(jnp.int32, (LANES, LANES), 1)
    is_gap = lax.broadcasted_iota(jnp.int32, (16, LANES), 0) % 8 < 5
    blank = jnp.zeros((16, LANES), BF)
    pad = jnp.zeros((96, LANES), BF)

    def run(q, place, *counts):
        for k in range(group):
            count = counts[k * len(counts) // group]
            if count == 0:
                continue
            b = q * LANES + place + k if first else table[q, place + k]
            features = pl.ds(pl.multiple_of(b * LANES, LANES), LANES)
            if first:
                own = own_tiles[pl.ds(pl.multiple_of(b * 8, 8), 8), :]
                high = own.astype(BF).astype(F32)
                twice = [jnp.concatenate([part, part], 0).astype(BF) for part in (high, own - high)]
                lhs = jnp.concatenate([*twice, pad], 0).T
                lhs_ref[features, :] = lhs
            else:
                lhs = lhs_ref[features, :]
            acc = None
            for p in range(count):
                mate = b if first else table[(2 + p) * halves + q, place + k]
                parts = split(mate_tiles[pl.ds(pl.multiple_of(mate * 8, 8), 8), :])
                sides = []
                for side in (jnp.where(is_gap, parts, blank), jnp.where(is_gap, blank, parts)):
                    sides.append(jnp.concatenate([side, side, pad], 0))
                both = jnp.dot(lhs, jnp.concatenate(sides, 1), preferred_element_type=F32)
                gap = jnp.maximum(both[:, :LANES], SPEED_FLOOR)
                term = both[:, LANES:] * (gap * lax.rsqrt(gap))
                acc = term if acc is None else acc + term
            total = jnp.broadcast_to(jnp.sum(acc, axis=1, keepdims=True), (LANES, LANES))
            at = pl.multiple_of(jnp.bitwise_and(b, -LANES), LANES)
            pltpu.store(cols.at[pl.ds(at, LANES), :], total, mask=lane == jnp.bitwise_and(b, LANES - 1))

    def step(g, carry):
        q = g // (LANES // group)
        place = (g % (LANES // group)) * group
        if first:
            run(q, place, 1)
            return carry
        longest = table[halves + q, place]
        second = table[halves + q, place + group // 2]
        second = jnp.where(longest > 1, jnp.maximum(second, 1), second)
        for one_half in range(1, most + 1):
            for other in range(0 if one_half == 1 else 1, one_half + 1):

                @pl.when((longest == one_half) & (second == other))
                def _():
                    run(q, place, one_half, other)

        return carry

    lax.fori_loop(0, blocks // group, step, 0)
    for h in range(halves):
        at = pl.ds(h * LANES, LANES)
        total = cols[at, :].T
        rad = own_ref[pl.ds(3 * blocks + h * LANES, LANES), :]
        wt = own_ref[pl.ds(4 * blocks + h * LANES, LANES), :]
        if first:
            total = total - (4.0 * SPEED_FLOOR**0.5) * wt * rad * rad
        else:
            total = total + prev_ref[at, :]
        if last:
            total = wt * total * (1.0 / (MOST * LANES))
        out_ref[at, :] = total
    if first:
        store_next.wait()


def pairs(own, mates, prev, lhs, own_too, last, resident, moved=None):
    rows = own.shape[0]
    blocks = rows // 5 // LANES * LANES
    first = prev is None
    most = MOST - 1
    units = sum(a.shape[0] for a in mates) // rows + (1 if first or own_too else 0)
    table = -(-(most + 2) * (blocks // LANES) // 8) * 8
    operands = [own, *mates, *((moved,) if first else (prev, lhs))]
    total = result((blocks, LANES), F32, resident and not last)
    vmem = pl.BlockSpec(memory_space=pltpu.VMEM)
    if first:
        features = result((blocks * LANES, LANES), BF, resident)
        out_shape = (total, features, jax.ShapeDtypeStruct(moved.shape, F32))
        out_specs = (vmem, vmem, pl.BlockSpec(memory_space=pltpu.HBM))
    else:
        out_shape, out_specs = total, vmem
    if resident:
        operands = [pltpu.with_memory_space_constraint(a, pltpu.VMEM) for a in operands]
    return pl.pallas_call(
        functools.partial(
            pairs_kernel,
            arrays=len(mates),
            first=first,
            last=last,
            own_too=own_too,
            most=most,
            group=64 if first else 32,
        ),
        in_specs=[vmem] * len(operands),
        out_specs=out_specs,
        out_shape=out_shape,
        scratch_shapes=[
            pltpu.VMEM((blocks * 8, LANES), F32),
            pltpu.VMEM(((units * blocks + 1) * 8, LANES), F32),
            pltpu.VMEM((blocks, LANES), F32),
            pltpu.VMEM((table, LANES), jnp.int32),
            pltpu.SMEM((table, LANES), jnp.int32),
            pltpu.SemaphoreType.DMA((1,)),
        ],
        compiler_params=pltpu.CompilerParams(vmem_limit_bytes=KERNEL_VMEM) if resident else None,
        name="pairs",
    )(*operands)


def exchange(own, size):
    def send(a, bit_of):
        return lax.ppermute(a, "space", [(i, i ^ bit_of(i)) for i in range(size)])

    def beside(i):
        return 1

    mate = send(own, beside)
    bits = [1 << k for k in range(1, size.bit_length() - 1)]
    if len(bits) == 2:
        def across(i):
            return bits[i % 2]

        far = send(own, across)
        far_mate = send(mate, across)
        far_beside = send(far, beside)
        corner = send(far_beside, across)
        far_mate_beside = send(far_mate, beside)
        corner_beside = send(corner, beside)
        return [[mate, far, far_beside], [far_mate, far_mate_beside, corner, corner_beside]]
    held = [own, mate]
    for bit in bits:
        held.append(send(jnp.concatenate(held, 0), lambda i: bit))
    return [[mate], held[2:]]


def on_device(orbit_state, object_props, density_table, block_cube):
    size = lax.axis_size("space")
    blocks = block_cube.shape[0]
    resident = size * unit_rows(blocks) * LANES * 4 <= KEPT_VMEM
    moved, own = propagate(density_table, orbit_state, object_props, block_cube, resident)
    groups = exchange(own, size)
    total, lhs, next_state = pairs(own, [], None, None, False, False, resident, moved)
    for k, mates in enumerate(groups):
        total = pairs(own, mates, total, lhs, k == 0, k == len(groups) - 1, resident)
    return (next_state, total.reshape(orbit_state.shape[1]))


def solution(mesh):
    placed = (P(None, ("mc", "space")), P(None, ("mc", "space")), P(), P(("mc", "space")))
    return jax.shard_map(
        on_device,
        mesh=mesh,
        in_specs=placed,
        out_specs=(P(None, ("mc", "space")), P(("mc", "space"))),
        check_vma=False,
    )
```
